256 devices in a mesh: rows: 32 (over x, z), mem: 8 (over y, core).
Axes of the slice: x: 4, y: 4, z: 8, core: 2. Of those that a mesh axis runs over, the one named last changes fastest.
Arguments:
- factor_panel: float32 [8, 32, 128, 2048], P(None, 'rows'), may hold values from -0.125 to 0.125
- right_side: float32 [8, 32, 128, 256], P(None, 'rows', None, 'mem'), may hold values from -6 to 6
- inverses: float32 [4, 512, 512], replicated, may hold values from -0.125 to 1.5, as said below
Outputs:
- solved: float32 [2048, 256], P(None, 'mem')
- remainder: float32 [8, 32, 128, 256], P(None, 'rows', None, 'mem')
- spread: float32 [8, 32, 128], P(None, 'rows')
The draws below stay inside these ranges and needn't reach their ends.
Inputs may be any that keep to these rules, and one draw needn't show every extreme that they name: `inverses`: each block is lower triangular with its diagonal between 0.5 and 1.5 and its entries below the diagonal between -0.125 and 0.125.
All inputs are finite; a program needn't handle non-finite values.
Results may differ from the reference program's by a relative error of at most 0.0001.
Values sent between devices are 32-bit elements; how exact they have to be, the bound alone decides.
No kernel may reach another device: no remote copies, remote signals or barrier semaphores. Data moves between devices by JAX's collectives and lax.ppermute only.
A program may use at most 64 MiB of HBM per device.

```python
import math
import jax
import jax.numpy as jnp
from jax import lax

TILE = 128
STEP_W = 512
STEPS = 4
TILE_BLOCKS = 8
COLS = 2048
MEMBERS = 256
N_ROWS = 32


def draw_inverses(key, part):
    diag_key, below_key = jax.random.split(jax.random.fold_in(key, 7))
    diagonal = jax.random.uniform(diag_key, (STEPS, STEP_W), jnp.float32, 0.5, 1.5)
    below = jnp.clip(jax.random.normal(below_key, (STEPS, STEP_W, STEP_W), jnp.float32), -4.0, 4.0)
    below = jnp.clip(below * (0.6 / math.sqrt(STEP_W)), -0.125, 0.125)
    below = jnp.tril(below, -1)
    identity = jnp.eye(STEP_W, dtype=jnp.float32)
    return below + identity[None] * diagonal[:, :, None]


def level_of(stream_key, shape, cuts, least, largest):
    def one(axis_at, shards_of):
        draws = jax.random.uniform(jax.random.fold_in(jax.random.fold_in(stream_key, 6), axis_at), (shards_of,), jnp.float32, least / len(cuts), largest / len(cuts))
        return jnp.repeat(jnp.exp(draws), shape[axis_at] // shards_of).reshape((-1,) + (1,) * (len(shape) - axis_at - 1))

    factor_of = one(*cuts[0])
    for cut in cuts[1:]:
        factor_of = factor_of * one(*cut)
    return factor_of


def noise(key, extent, scale, bound, cuts=(), kind=jnp.bfloat16):
    result = jax.random.normal(key, extent, jnp.float32) * scale
    if len(cuts) > 0:
        result = level_of(key, extent, cuts, -0.22, 0.18) * result
    return jnp.clip(result, min=-bound, max=bound).astype(kind)


def setup_inputs(seed: int = 0) -> dict:
    key_list = jax.random.split(jax.random.key(seed), 4)
    return {
        "factor_panel": noise(key_list[0], (TILE_BLOCKS, N_ROWS, TILE, COLS), COLS ** -0.5, 0.125, ((1, 32),), jnp.float32),
        "right_side": noise(key_list[1], (TILE_BLOCKS, N_ROWS, TILE, MEMBERS), 1.0, 6.0, ((1, 32), (3, 8)), jnp.float32),
        "inverses": draw_inverses(jax.random.fold_in(key_list[3], 71), 0),
    }


highest = lax.Precision.HIGHEST


def reference(factor_panel, right_side, inverses):
    lower_rows = factor_panel.reshape(-1, COLS)
    right_rows = right_side.reshape(-1, MEMBERS)
    row_ids = jnp.arange(COLS, dtype=jnp.int32)
    limits = (row_ids // STEP_W) * STEP_W
    column_ids = jnp.arange(COLS, dtype=jnp.int32)
    masked_head = jnp.where(column_ids[None, :] < limits[:, None], lower_rows[:COLS], jnp.float32(0.0))
    blocks = []
    for section in range(STEPS):
        start = section * STEP_W
        residual = right_rows[start:start + STEP_W]
        if section > 0:
            earlier = jnp.concatenate(blocks, axis=0)
            residual = residual - jnp.dot(masked_head[start:start + STEP_W, :start], earlier, precision=highest, preferred_element_type=jnp.float32)
        blocks.append(jnp.dot(inverses[section], residual, precision=highest, preferred_element_type=jnp.float32))
    solved = jnp.concatenate(blocks, axis=0)
    head_left = right_rows[:COLS] - jnp.dot(masked_head, solved, precision=highest, preferred_element_type=jnp.float32)
    tail_left = right_rows[COLS:] - jnp.dot(lower_rows[COLS:], solved, precision=highest, preferred_element_type=jnp.float32)
    remainder = jnp.concatenate([head_left, tail_left], axis=0)
    member_mean = jnp.sum(remainder, axis=1) / MEMBERS
    spread = jnp.sum(remainder * remainder, axis=1) / MEMBERS - member_mean * member_mean
    return solved, remainder.reshape(right_side.shape), spread.reshape(TILE_BLOCKS, N_ROWS, TILE)
```

```python
import jax
import jax.numpy as jnp
from jax import lax
from jax.sharding import Mesh, PartitionSpec as P

highest = lax.Precision.HIGHEST
AXES = ("xh", "xl", "zh", "zl", "y", "core")
SIZES = (2, 2, 2, 4, 4, 2)
ROWS = AXES[:4]
OWNERS = AXES[1:4]
MEM = AXES[4:]
TILES = 4
STEPS = 4


def spread_tile(tile, axes, count):
    copies = jnp.broadcast_to(tile[None], (count,) + tile.shape)
    return lax.all_to_all(copies, axes, 0, 0)


def times_rows(left, right):
    return lax.dot_general(
        left, right, (((1,), (1,)), ((), ())),
        precision=highest, preferred_element_type=jnp.float32,
    )


def side_by_side(tiles):
    count, members, rows = tiles.shape
    return tiles.transpose(1, 0, 2).reshape(members, count * rows)


def shards(factor_panel, right_side, inverses):
    blocks, _, rows, columns = factor_panel.shape
    members = right_side.shape[3]
    width = inverses.shape[1]
    panel = factor_panel.reshape(blocks, rows, columns)
    right = right_side.reshape(blocks, rows, members).transpose(0, 2, 1)
    tile = lax.axis_index(ROWS)
    step_of = tile // TILES
    is_head = step_of < STEPS

    own = right[0]
    for step in range(STEPS - 1):
        tiles = spread_tile(own, OWNERS, 16)
        residual = side_by_side(tiles[step * TILES:(step + 1) * TILES])
        solved = times_rows(residual, inverses[step])
        change = times_rows(solved, panel[0, :, step * width:(step + 1) * width])
        own = jnp.where(is_head & (step < step_of), own - change, own)

    tiles = spread_tile(own, ROWS, 32)[:STEPS * TILES]
    residual = side_by_side(tiles).reshape(members, STEPS, width)
    solved = jnp.concatenate(
        [times_rows(residual[:, step], inverses[step]) for step in range(STEPS)], axis=1
    )
    product = times_rows(solved, panel.reshape(blocks * rows, columns))
    product = product.reshape(members, blocks, rows).transpose(1, 0, 2)
    left = right - product
    left = left.at[0].set(jnp.where(is_head, own, left[0]))

    sums = jnp.stack([jnp.sum(left, axis=1), jnp.sum(left * left, axis=1)])
    sums = jnp.sum(spread_tile(sums, MEM, 8), axis=0)
    count = members * 8
    mean = sums[0] / count
    spread = sums[1] / count - mean * mean
    return (
        solved.T,
        left.transpose(0, 2, 1).reshape(right_side.shape),
        spread.reshape(blocks, 1, rows),
    )


def solution(mesh):
    fine = Mesh(mesh.devices.reshape(SIZES), AXES)
    return jax.shard_map(
        shards,
        mesh=fine,
        in_specs=(P(None, ROWS, None, None), P(None, ROWS, None, MEM), P()),
        out_specs=(P(None, MEM), P(None, ROWS, None, MEM), P(None, ROWS, None)),
        check_vma=False,
    )
```

```python
import jax
import jax.numpy as jnp
from jax import lax
from jax.experimental import pallas as pl
from jax.experimental.pallas import tpu as pltpu
from jax.sharding import Mesh, PartitionSpec as P

highest = lax.Precision.HIGHEST
f32 = jnp.float32
bf16 = jnp.bfloat16
AXES = ("xh", "xl", "zh", "zl", "y", "core")
SIZES = (2, 2, 2, 4, 4, 2)
ROWS = AXES[:4]
OWNERS = AXES[1:4]
MEM = AXES[4:]
TILES = 4
STEPS = 4
WIDTH = 512
ROW = 128
NT = (((1,), (1,)), ((), ()))
NN = (((1,), (0,)), ((), ()))


def dot32(left, right, dims):
    return lax.dot_general(left, right, dims, precision=highest, preferred_element_type=f32)


def split(value):
    high = value.astype(bf16)
    return high, (value - high.astype(f32)).astype(bf16)


def dot16(left, right, dims):
    return lax.dot_general(left, right, dims, preferred_element_type=f32)


def joined(ref, step):
    return jnp.concatenate([ref[step * TILES + i] for i in range(TILES)], axis=1)


def prepare_body(count_ref, panel_ref, inverses_ref, factor_ref, panel_high_ref,
                 panel_low_ref, inverse_high_ref, inverse_low_ref):
    for block in range(panel_ref.shape[0]):
        panel_high_ref[block], panel_low_ref[block] = split(panel_ref[block])
    for step in range(STEPS):
        inverse_high_ref[step], inverse_low_ref[step] = split(inverses_ref[step])
    for step in range(STEPS - 1):
        part = panel_ref[0, :, step * WIDTH:(step + 1) * WIDTH]
        part = jnp.where(count_ref[0] > step, part, 0.0)
        factor_ref[step] = dot32(part, inverses_ref[step], NN)


def round_body(step, tiles_ref, own_ref, factor_ref, copies_ref, own_out_ref):
    change = dot32(joined(tiles_ref, step), factor_ref[step], NT)
    own = own_ref[...] - change
    own_out_ref[...] = own
    for i in range(copies_ref.shape[0]):
        copies_ref[i] = own


def times_split(value, high_ref, low_ref, at):
    rows = value.shape[0]
    high, low = split(value)
    wide = dot16(jnp.concatenate([high, low], axis=0), high_ref[at], NT)
    return wide[:rows] + wide[rows:] + dot16(high, low_ref[at], NT)


def finish_body(count_ref, tiles_ref, own_ref, right_ref, panel_high_ref, panel_low_ref,
                inverse_high_ref, inverse_low_ref, solved_ref, left_ref, sums_ref):
    parts = []
    for step in range(STEPS):
        solved = times_split(joined(tiles_ref, step), inverse_high_ref, inverse_low_ref, step)
        solved_ref[:, step * WIDTH:(step + 1) * WIDTH] = solved
        parts.append(solved)
    solved = jnp.concatenate(parts, axis=1)
    for block in range(right_ref.shape[0]):
        left = right_ref[block] - times_split(solved, panel_high_ref, panel_low_ref, block)
        if block == 0:
            left = jnp.where(count_ref[0] >= 0, own_ref[...], left)
        left_ref[block] = left
        total = jnp.sum(left, axis=0, keepdims=True)
        square = jnp.sum(left * left, axis=0, keepdims=True)
        for i in range(8):
            sums_ref[i, 0, block:block + 1] = total
            sums_ref[i, 1, block:block + 1] = square


VMEM = pl.BlockSpec(memory_space=pltpu.VMEM)
SMEM = pl.BlockSpec(memory_space=pltpu.SMEM)


def shape(*dims):
    return jax.ShapeDtypeStruct(dims, f32)


def params(limit):
    return pltpu.CompilerParams(vmem_limit_bytes=limit << 20)


def cost(flops, size):
    return pl.CostEstimate(flops=flops, bytes_accessed=size, transcendentals=0)


def prepare(count, panel, inverses):
    halves = [jax.ShapeDtypeStruct(panel.shape, bf16)] * 2
    halves += [jax.ShapeDtypeStruct(inverses.shape, bf16)] * 2
    return pl.pallas_call(
        prepare_body,
        out_shape=[shape(STEPS - 1, ROW, WIDTH)] + halves,
        in_specs=[SMEM, VMEM, VMEM],
        out_specs=[VMEM] * 5,
        compiler_params=params(32),
        cost_estimate=cost(6 * 3 * 2 * ROW * WIDTH * WIDTH, 24 << 20),
        name="prepare",
    )(count, panel, inverses)


def advance(step, copies, tiles, own, factor):
    members = own.shape[0]
    return pl.pallas_call(
        lambda *refs: round_body(step, *refs),
        out_shape=(shape(copies, members, ROW), shape(members, ROW)),
        in_specs=[VMEM] * 3,
        out_specs=(VMEM, VMEM),
        compiler_params=params(8),
        name=f"advance{step}",
    )(tiles, own, factor)


def finish(count, tiles, own, right, halves):
    blocks, members, rows = right.shape
    return pl.pallas_call(
        finish_body,
        out_shape=(shape(members, STEPS * WIDTH), shape(blocks, members, rows),
                   shape(8, 2, blocks, rows)),
        in_specs=[SMEM] + [VMEM] * 7,
        out_specs=(VMEM, VMEM, VMEM),
        compiler_params=params(24),
        name="finish",
    )(count, tiles, own, right, *halves)


def shards(factor_panel, right_side, inverses):
    blocks, _, rows, columns = factor_panel.shape
    members = right_side.shape[3]
    panel = factor_panel.reshape(blocks, rows, columns)
    right = right_side.reshape(blocks, rows, members).transpose(0, 2, 1)
    step_of = lax.axis_index(ROWS) // TILES
    count = jnp.where(step_of < STEPS, step_of, -1).astype(jnp.int32).reshape(1)

    own = right[0]
    copies = jnp.broadcast_to(own[None], (16,) + own.shape)
    factor, *halves = prepare(count, panel, inverses)
    for step in range(STEPS - 1):
        tiles = lax.all_to_all(copies, OWNERS, 0, 0)
        copies, own = advance(step, 16 if step < STEPS - 2 else 32, tiles, own, factor)
    tiles = lax.all_to_all(copies, ROWS, 0, 0)
    solved, left, sums = finish(count, tiles, own, right, halves)
    sums = jnp.sum(lax.all_to_all(sums, MEM, 0, 0), axis=0)
    size = members * 8
    mean = sums[0] / size
    spread = sums[1] / size - mean * mean
    return (
        solved.T,
        left.transpose(0, 2, 1).reshape(right_side.shape),
        spread.reshape(blocks, 1, rows),
    )


def solution(mesh):
    fine = Mesh(mesh.devices.reshape(SIZES), AXES)
    return jax.shard_map(
        shards,
        mesh=fine,
        in_specs=(P(None, ROWS, None, None), P(None, ROWS, None, MEM), P()),
        out_specs=(P(None, MEM), P(None, ROWS, None, MEM), P(None, ROWS, None)),
        check_vma=False,
    )
```

```python
import jax
import jax.numpy as jnp
from jax import lax
from jax.experimental import pallas as pl
from jax.experimental.pallas import tpu as pltpu
from jax.sharding import Mesh, PartitionSpec as P

highest = lax.Precision.HIGHEST
f32 = jnp.float32
bf16 = jnp.bfloat16
AXES = ("xh", "xl", "zh", "zl", "y", "core")
SIZES = (2, 2, 2, 4, 4, 2)
ROWS = AXES[:4]
OWNERS = AXES[1:4]
MEM = AXES[4:]
TILES = 4
STEPS = 4
WIDTH = 512
ROW = 128
NT = (((1,), (1,)), ((), ()))
NN = (((1,), (0,)), ((), ()))


def dot32(left, right, dims):
    return lax.dot_general(left, right, dims, precision=highest, preferred_element_type=f32)


def split(value):
    high = value.astype(bf16)
    return high, (value - high.astype(f32)).astype(bf16)


def dot16(left, right, dims):
    return lax.dot_general(left, right, dims, preferred_element_type=f32)


def joined(ref, step):
    return jnp.concatenate([ref[step * TILES + i] for i in range(TILES)], axis=1)


def times_split(value, right):
    rows = value.shape[0]
    high, low = split(value)
    right_high, right_low = split(right)
    wide = dot16(jnp.concatenate([high, low], axis=0), right_high, NT)
    return wide[:rows] + wide[rows:] + dot16(high, right_low, NT)


def begin_body(right_ref, copies_ref, own_ref):
    own = right_ref[0]
    own_ref[...] = own
    for i in range(copies_ref.shape[0]):
        copies_ref[i] = own


def advance_body(step, count_ref, tiles_ref, own_ref, panel_ref, inverses_ref,
                 copies_ref, own_out_ref):
    solved = dot32(joined(tiles_ref, step), inverses_ref[step], NT)
    change = dot32(solved, panel_ref[0, :, step * WIDTH:(step + 1) * WIDTH], NT)
    own = jnp.where(count_ref[0] > step, own_ref[...] - change, own_ref[...])
    own_out_ref[...] = own
    for i in range(copies_ref.shape[0]):
        copies_ref[i] = own


def finish_body(count_ref, tiles_ref, own_ref, right_ref, panel_ref, inverses_ref,
                solved_ref, left_ref, sums_ref):
    parts = []
    for step in range(STEPS):
        solved = times_split(joined(tiles_ref, step), inverses_ref[step])
        solved_ref[:, step * WIDTH:(step + 1) * WIDTH] = solved
        parts.append(solved)
    solved = jnp.concatenate(parts, axis=1)
    for block in range(right_ref.shape[0]):
        left = right_ref[block] - times_split(solved, panel_ref[block])
        if block == 0:
            left = jnp.where(count_ref[0] >= 0, own_ref[...], left)
        left_ref[block] = left
        total = jnp.sum(left, axis=0, keepdims=True)
        square = jnp.sum(left * left, axis=0, keepdims=True)
        for i in range(8):
            sums_ref[i, 0, block:block + 1] = total
            sums_ref[i, 1, block:block + 1] = square


VMEM = pl.BlockSpec(memory_space=pltpu.VMEM)
SMEM = pl.BlockSpec(memory_space=pltpu.SMEM)


def shape(*dims):
    return jax.ShapeDtypeStruct(dims, f32)


def params(limit):
    return pltpu.CompilerParams(vmem_limit_bytes=limit << 20)


def cost(flops, size):
    return pl.CostEstimate(flops=flops, bytes_accessed=size, transcendentals=0)


def local(body, name, limit, outs, flops, size, *args):
    smem = [SMEM] if args[0].ndim == 1 else []
    return pl.pallas_call(
        body,
        out_shape=outs,
        in_specs=smem + [VMEM] * (len(args) - len(smem)),
        out_specs=[VMEM] * len(outs),
        compiler_params=params(limit),
        cost_estimate=cost(flops, size),
        name=name,
    )(*args)


def shards(factor_panel, right_side, inverses):
    blocks, _, rows, columns = factor_panel.shape
    members = right_side.shape[3]
    panel = factor_panel.reshape(blocks, rows, columns)
    right = right_side.reshape(blocks, rows, members).transpose(0, 2, 1)
    step_of = lax.axis_index(ROWS) // TILES
    count = jnp.where(step_of < STEPS, step_of, -1).astype(jnp.int32).reshape(1)
    tile = shape(members, rows)
    group = shape(16, members, rows)
    every = shape(32, members, rows)

    right, count = lax.optimization_barrier((right, count))
    copies, own = local(begin_body, "begin", 8, [group, tile], 1 << 34, 1 << 20, right)
    for step in range(STEPS - 1):
        last = step == STEPS - 2
        tiles = lax.all_to_all(copies, OWNERS, 0, 0)
        copies, own = local(
            lambda *refs, step=step: advance_body(step, *refs), f"advance{step}", 8,
            [every if last else group, tile], 1 << 28, 2 << 20,
            count, tiles, own, panel, inverses,
        )
    tiles = lax.all_to_all(copies, ROWS, 0, 0)
    solved, left, sums = local(
        finish_body, "finish", 16,
        [shape(members, STEPS * WIDTH), shape(blocks, members, rows), shape(8, 2, blocks, rows)],
        1 << 30, 12 << 20, count, tiles, own, right, panel, inverses,
    )
    sums = jnp.sum(lax.all_to_all(sums, MEM, 0, 0), axis=0)
    size = members * 8
    mean = sums[0] / size
    spread = sums[1] / size - mean * mean
    return (
        solved.T,
        left.transpose(0, 2, 1).reshape(right_side.shape),
        spread.reshape(blocks, 1, rows),
    )


def solution(mesh):
    fine = Mesh(mesh.devices.reshape(SIZES), AXES)
    return jax.shard_map(
        shards,
        mesh=fine,
        in_specs=(P(None, ROWS, None, None), P(None, ROWS, None, MEM), P()),
        out_specs=(P(None, MEM), P(None, ROWS, None, MEM), P(None, ROWS, None)),
        check_vma=False,
    )
```

```python
import jax
import jax.numpy as jnp
from jax import lax
from jax.experimental import pallas as pl
from jax.experimental.pallas import tpu as pltpu
from jax.sharding import Mesh, PartitionSpec as P

f32 = jnp.float32
bf16 = jnp.bfloat16
AXES = ("xh", "xl", "zh", "zl", "y", "core")
SIZES = (2, 2, 2, 4, 4, 2)
ROWS = AXES[:4]
OWNERS = AXES[1:4]
MEM = AXES[4:]
TILES = 4
STEPS = 4
WIDTH = 512
NT = (((1,), (1,)), ((), ()))
SOURCES = 4
GROUP = (OWNERS, OWNERS, ROWS[2:], ROWS[2:])
NUMBER = (16, 16, 8, 8)
FIRST = (0, 4, 0, 4)


def FINAL(step):
    return step == STEPS - 2


def line_of():
    return jnp.bitwise_xor(lax.axis_index(ROWS[:2]), 1)


def crossings(value):
    return [
        lax.ppermute(value, ROWS[:2], [(i, i ^ change) for i in range(4)])
        for change in (1, 2, 3)
    ]


def split(value):
    high = value.astype(bf16)
    return high, (value - high.astype(f32)).astype(bf16)


def dot16(left, right, dims):
    return lax.dot_general(left, right, dims, preferred_element_type=f32)


def joined(ref, first):
    return jnp.concatenate([ref[first + i] for i in range(TILES)], axis=1)


def times_split(value, right):
    rows = value.shape[0]
    high, low = split(value)
    right_high, right_low = split(right)
    wide = dot16(jnp.concatenate([high, low], axis=0), right_high, NT)
    return wide[:rows] + wide[rows:] + dot16(high, right_low, NT)


def chosen(line, refs, first):
    value = joined(refs[0], first)
    for at, ref in enumerate(refs[1:]):
        value = jnp.where(line == at + 1, joined(ref, first), value)
    return value


def begin_body(right_ref, copies_ref, own_ref):
    own = right_ref[0]
    own_ref[...] = own
    for i in range(copies_ref.shape[0]):
        copies_ref[i] = own


def advance_body(step, count_ref, *refs):
    outs = refs[-3:] if FINAL(step) else refs[-2:]
    *tiles, own_ref, panel_ref, inverses_ref = refs[:-len(outs)]
    solved = times_split(joined(tiles[-1], FIRST[step]), inverses_ref[step])
    change = times_split(solved, panel_ref[0, :, step * WIDTH:(step + 1) * WIDTH])
    own = jnp.where(count_ref[0] > step, own_ref[...] - change, own_ref[...])
    outs[1][...] = own
    for i in range(outs[0].shape[0]):
        outs[0][i] = own
    if FINAL(step):
        for at, ref in enumerate(tiles):
            for i in range(TILES):
                outs[2][at * TILES + i] = ref[FIRST[at] + i]


def middle_body(count_ref, *refs):
    sources = refs[:SOURCES]
    right_ref, panel_ref, inverses_ref = refs[SOURCES:SOURCES + 3]
    solved_ref, left_ref = refs[-2:]
    parts = []
    for step in range(STEPS - 1):
        solved = times_split(chosen(count_ref[1], sources, step * TILES), inverses_ref[step])
        solved_ref[:, step * WIDTH:(step + 1) * WIDTH] = solved
        parts.append(solved)
    solved = jnp.concatenate(parts, axis=1)
    for block in range(right_ref.shape[0]):
        product = times_split(solved, panel_ref[block, :, :(STEPS - 1) * WIDTH])
        left_ref[block] = right_ref[block] - product


def finish_body(count_ref, *refs):
    sources = refs[:SOURCES]
    own_ref, partly_ref, before_ref, panel_ref, inverses_ref = refs[SOURCES:SOURCES + 5]
    solved_ref, left_ref, sums_ref = refs[-3:]
    step = STEPS - 1
    solved = times_split(chosen(count_ref[1], sources, 0), inverses_ref[step])
    solved_ref[:, :step * WIDTH] = before_ref[...]
    solved_ref[:, step * WIDTH:] = solved
    for block in range(partly_ref.shape[0]):
        product = times_split(solved, panel_ref[block, :, step * WIDTH:])
        left = partly_ref[block] - product
        if block == 0:
            left = jnp.where(count_ref[0] >= 0, own_ref[...], left)
        left_ref[block] = left
        total = jnp.sum(left, axis=0, keepdims=True)
        square = jnp.sum(left * left, axis=0, keepdims=True)
        for i in range(8):
            sums_ref[i, 0, block:block + 1] = total
            sums_ref[i, 1, block:block + 1] = square


VMEM = pl.BlockSpec(memory_space=pltpu.VMEM)
SMEM = pl.BlockSpec(memory_space=pltpu.SMEM)


def shape(*dims):
    return jax.ShapeDtypeStruct(dims, f32)


def params(limit):
    return pltpu.CompilerParams(vmem_limit_bytes=limit << 20)


def cost(flops, size):
    return pl.CostEstimate(flops=flops, bytes_accessed=size, transcendentals=0)


def local(body, limit, outs, flops, size, *args):
    smem = [SMEM] if args[0].ndim == 1 else []
    return pl.pallas_call(
        body,
        out_shape=outs,
        in_specs=smem + [VMEM] * (len(args) - len(smem)),
        out_specs=[VMEM] * len(outs),
        compiler_params=params(limit),
        cost_estimate=cost(flops, size),
    )(*args)


def shards(factor_panel, right_side, inverses):
    blocks, _, rows, columns = factor_panel.shape
    members = right_side.shape[3]
    panel = factor_panel.reshape(blocks, rows, columns)
    right = right_side.reshape(blocks, rows, members).transpose(0, 2, 1)
    step_of = lax.axis_index(ROWS) // TILES
    count = jnp.stack([jnp.where(step_of < STEPS, step_of, -1), line_of()]).astype(jnp.int32)
    tile = shape(members, rows)
    right, count = lax.optimization_barrier((right, count))

    copies, own = local(
        begin_body, 8, [shape(NUMBER[0], members, rows), tile], 1 << 34, 1 << 20, right
    )
    received = []
    for step in range(STEPS - 1):
        received.append(lax.all_to_all(copies, GROUP[step], 0, 0))
        outs = [shape(NUMBER[step + 1], members, rows), tile]
        tiles = received[-1:]
        if FINAL(step):
            tiles = received
            outs.append(shape(3 * TILES, members, rows))
        copies, own, *packed = local(
            lambda *refs, step=step: advance_body(step, *refs), 8, outs,
            1 << 28, 2 << 20, count, *tiles, own, panel, inverses,
        )
    early = crossings(packed[0])
    received = lax.all_to_all(copies, GROUP[STEPS - 1], 0, 0)
    ends = received[FIRST[STEPS - 1]:FIRST[STEPS - 1] + TILES]
    late = crossings(ends)
    own, ends, *early = lax.optimization_barrier((own, ends, packed[0], *early))
    before, partly = local(
        middle_body, 16,
        [shape(members, (STEPS - 1) * WIDTH), shape(blocks, members, rows)],
        1 << 30, 12 << 20, count, *early, right, panel, inverses,
    )
    solved, left, sums = local(
        finish_body, 16,
        [shape(members, STEPS * WIDTH), shape(blocks, members, rows), shape(8, 2, blocks, rows)],
        1 << 28, 4 << 20, count, ends, *late, own, partly, before, panel, inverses,
    )
    sums = jnp.sum(lax.all_to_all(sums, MEM, 0, 0), axis=0)
    size = members * 8
    mean = sums[0] / size
    spread = sums[1] / size - mean * mean
    return (
        solved.T,
        left.transpose(0, 2, 1).reshape(right_side.shape),
        spread.reshape(blocks, 1, rows),
    )


def solution(mesh):
    fine = Mesh(mesh.devices.reshape(SIZES), AXES)
    return jax.shard_map(
        shards,
        mesh=fine,
        in_specs=(P(None, ROWS, None, None), P(None, ROWS, None, MEM), P()),
        out_specs=(P(None, MEM), P(None, ROWS, None, MEM), P(None, ROWS, None)),
        check_vma=False,
    )
```

```python
import jax
import jax.numpy as jnp
from jax import lax
from jax.experimental import pallas as pl
from jax.experimental.pallas import tpu as pltpu
from jax.sharding import Mesh, PartitionSpec as P

f32 = jnp.float32
bf16 = jnp.bfloat16
AXES = ("xh", "xl", "zh", "zl", "y", "core")
SIZES = (2, 2, 2, 4, 4, 2)
ROWS = AXES[:4]
OWNERS = AXES[1:4]
MEM = AXES[4:]
TILES = 4
STEPS = 4
WIDTH = 512
NT = (((1,), (1,)), ((), ()))
SOURCES = 2
GROUP = (OWNERS,) * STEPS
NUMBER = (16,) * STEPS
FIRST = (0, 4, 8, 12)


def FINAL(step):
    return step == STEPS - 2


def line_of():
    return lax.axis_index("xh")


def crossings(value):
    return [lax.ppermute(value, "xh", [(0, 1), (1, 0)])]


def split(value):
    high = value.astype(bf16)
    return high, (value - high.astype(f32)).astype(bf16)


def dot16(left, right, dims):
    return lax.dot_general(left, right, dims, preferred_element_type=f32)


def joined(ref, first):
    return jnp.concatenate([ref[first + i] for i in range(TILES)], axis=1)


def times_split(value, right):
    rows = value.shape[0]
    high, low = split(value)
    right_high, right_low = split(right)
    wide = dot16(jnp.concatenate([high, low], axis=0), right_high, NT)
    return wide[:rows] + wide[rows:] + dot16(high, right_low, NT)


def chosen(line, refs, first):
    value = joined(refs[0], first)
    for at, ref in enumerate(refs[1:]):
        value = jnp.where(line == at + 1, joined(ref, first), value)
    return value


def begin_body(right_ref, copies_ref, own_ref):
    own = right_ref[0]
    own_ref[...] = own
    for i in range(copies_ref.shape[0]):
        copies_ref[i] = own


def advance_body(step, count_ref, *refs):
    outs = refs[-3:] if FINAL(step) else refs[-2:]
    *tiles, own_ref, panel_ref, inverses_ref = refs[:-len(outs)]
    solved = times_split(joined(tiles[-1], FIRST[step]), inverses_ref[step])
    change = times_split(solved, panel_ref[0, :, step * WIDTH:(step + 1) * WIDTH])
    own = jnp.where(count_ref[0] > step, own_ref[...] - change, own_ref[...])
    outs[1][...] = own
    for i in range(outs[0].shape[0]):
        outs[0][i] = own
    if FINAL(step):
        for at, ref in enumerate(tiles):
            for i in range(TILES):
                outs[2][at * TILES + i] = ref[FIRST[at] + i]


def middle_body(count_ref, *refs):
    sources = refs[:SOURCES]
    right_ref, panel_ref, inverses_ref = refs[SOURCES:SOURCES + 3]
    solved_ref, left_ref = refs[-2:]
    parts = []
    for step in range(STEPS - 1):
        solved = times_split(chosen(count_ref[1], sources, step * TILES), inverses_ref[step])
        solved_ref[:, step * WIDTH:(step + 1) * WIDTH] = solved
        parts.append(solved)
    solved = jnp.concatenate(parts, axis=1)
    for block in range(right_ref.shape[0]):
        product = times_split(solved, panel_ref[block, :, :(STEPS - 1) * WIDTH])
        left_ref[block] = right_ref[block] - product


def finish_body(count_ref, *refs):
    sources = refs[:SOURCES]
    own_ref, partly_ref, before_ref, panel_ref, inverses_ref = refs[SOURCES:SOURCES + 5]
    solved_ref, left_ref, sums_ref = refs[-3:]
    step = STEPS - 1
    solved = times_split(chosen(count_ref[1], sources, 0), inverses_ref[step])
    solved_ref[:, :step * WIDTH] = before_ref[...]
    solved_ref[:, step * WIDTH:] = solved
    for block in range(partly_ref.shape[0]):
        product = times_split(solved, panel_ref[block, :, step * WIDTH:])
        left = partly_ref[block] - product
        if block == 0:
            left = jnp.where(count_ref[0] >= 0, own_ref[...], left)
        left_ref[block] = left
        total = jnp.sum(left, axis=0, keepdims=True)
        square = jnp.sum(left * left, axis=0, keepdims=True)
        for i in range(8):
            sums_ref[i, 0, block:block + 1] = total
            sums_ref[i, 1, block:block + 1] = square


VMEM = pl.BlockSpec(memory_space=pltpu.VMEM)
SMEM = pl.BlockSpec(memory_space=pltpu.SMEM)


def shape(*dims):
    return jax.ShapeDtypeStruct(dims, f32)


def params(limit):
    return pltpu.CompilerParams(vmem_limit_bytes=limit << 20)


def cost(flops, size):
    return pl.CostEstimate(flops=flops, bytes_accessed=size, transcendentals=0)


def local(body, limit, outs, flops, size, *args):
    smem = [SMEM] if args[0].ndim == 1 else []
    return pl.pallas_call(
        body,
        out_shape=outs,
        in_specs=smem + [VMEM] * (len(args) - len(smem)),
        out_specs=[VMEM] * len(outs),
        compiler_params=params(limit),
        cost_estimate=cost(flops, size),
    )(*args)


def shards(factor_panel, right_side, inverses):
    blocks, _, rows, columns = factor_panel.shape
    members = right_side.shape[3]
    panel = factor_panel.reshape(blocks, rows, columns)
    right = right_side.reshape(blocks, rows, members).transpose(0, 2, 1)
    step_of = lax.axis_index(ROWS) // TILES
    count = jnp.stack([jnp.where(step_of < STEPS, step_of, -1), line_of()]).astype(jnp.int32)
    tile = shape(members, rows)
    right, count = lax.optimization_barrier((right, count))

    copies, own = local(
        begin_body, 8, [shape(NUMBER[0], members, rows), tile], 1 << 34, 1 << 20, right
    )
    received = []
    for step in range(STEPS - 1):
        received.append(lax.all_to_all(copies, GROUP[step], 0, 0))
        outs = [shape(NUMBER[step + 1], members, rows), tile]
        tiles = received[-1:]
        if FINAL(step):
            tiles = received
            outs.append(shape(3 * TILES, members, rows))
        copies, own, *packed = local(
            lambda *refs, step=step: advance_body(step, *refs), 8, outs,
            1 << 28, 2 << 20, count, *tiles, own, panel, inverses,
        )
    early = crossings(packed[0])
    received = lax.all_to_all(copies, GROUP[STEPS - 1], 0, 0)
    ends = received[FIRST[STEPS - 1]:FIRST[STEPS - 1] + TILES]
    late = crossings(ends)
    own, ends, *early = lax.optimization_barrier((own, ends, packed[0], *early))
    before, partly = local(
        middle_body, 16,
        [shape(members, (STEPS - 1) * WIDTH), shape(blocks, members, rows)],
        1 << 30, 12 << 20, count, *early, right, panel, inverses,
    )
    solved, left, sums = local(
        finish_body, 16,
        [shape(members, STEPS * WIDTH), shape(blocks, members, rows), shape(8, 2, blocks, rows)],
        1 << 28, 4 << 20, count, ends, *late, own, partly, before, panel, inverses,
    )
    sums = jnp.sum(lax.all_to_all(sums, MEM, 0, 0), axis=0)
    size = members * 8
    mean = sums[0] / size
    spread = sums[1] / size - mean * mean
    return (
        solved.T,
        left.transpose(0, 2, 1).reshape(right_side.shape),
        spread.reshape(blocks, 1, rows),
    )


def solution(mesh):
    fine = Mesh(mesh.devices.reshape(SIZES), AXES)
    return jax.shard_map(
        shards,
        mesh=fine,
        in_specs=(P(None, ROWS, None, None), P(None, ROWS, None, MEM), P()),
        out_specs=(P(None, MEM), P(None, ROWS, None, MEM), P(None, ROWS, None)),
        check_vma=False,
    )
```

```python
import jax
import jax.numpy as jnp
from jax import lax
from jax.experimental import pallas as pl
from jax.experimental.pallas import tpu as pltpu
from jax.sharding import Mesh, PartitionSpec as P

f32 = jnp.float32
bf16 = jnp.bfloat16
AXES = ("xh", "xl", "zh", "zl", "y", "core")
SIZES = (2, 2, 2, 4, 4, 2)
ROWS = AXES[:4]
OWNERS = AXES[1:4]
MEM = AXES[4:]
TILES = 4
STEPS = 4
WIDTH = 512
NT = (((1,), (1,)), ((), ()))
NN = (((1,), (0,)), ((), ()))
SOURCES = 2
GROUP = 16


def line_of():
    return lax.axis_index("xh")


def crossings(value):
    return [lax.ppermute(value, "xh", [(0, 1), (1, 0)])]


def split(value):
    high = value.astype(bf16)
    return high, (value - high.astype(f32)).astype(bf16)


def dot16(left, right, dims):
    return lax.dot_general(left, right, dims, preferred_element_type=f32)


def joined(ref, first):
    return jnp.concatenate([ref[first + i] for i in range(TILES)], axis=1)


def times_split(value, right):
    rows = value.shape[0]
    high, low = split(value)
    right_high, right_low = split(right)
    wide = dot16(jnp.concatenate([high, low], axis=0), right_high, NT)
    return wide[:rows] + wide[rows:] + dot16(high, right_low, NT)


def chosen(line, refs, first):
    value = joined(refs[0], first)
    for at, ref in enumerate(refs[1:]):
        value = jnp.where(line == at + 1, joined(ref, first), value)
    return value


def begin_body(right_ref, own_ref):
    own_ref[...] = right_ref[0]


def prepare_body(panel_ref, inverses_ref, factor_ref):
    for step in range(STEPS - 1):
        part = panel_ref[0, :, step * WIDTH:(step + 1) * WIDTH]
        factor_ref[:, step * WIDTH:(step + 1) * WIDTH] = lax.dot_general(
            part, inverses_ref[step], NN, precision=lax.Precision.HIGHEST,
            preferred_element_type=f32,
        )


def arrived(lane, refs, at):
    tiles = []
    for tile in range(TILES):
        wanted = jnp.bitwise_xor(lane, tile)
        value = refs[0][at]
        for change in range(1, TILES):
            value = jnp.where(wanted == change, refs[change][at], value)
        tiles.append(value)
    return tiles


def advanced(count_ref, own_ref, factor_ref, tiles):
    steps = len(tiles) // TILES
    change = times_split(jnp.concatenate(tiles, axis=1), factor_ref[:, :steps * WIDTH])
    return jnp.where(count_ref[0] == steps, own_ref[...] - change, own_ref[...])


def first_body(count_ref, r0, r1, r2, r3, own_ref, factor_ref, own_out_ref):
    own = advanced(count_ref, own_ref, factor_ref, arrived(count_ref[2], (r0, r1, r2, r3), 0))
    own_out_ref[0] = own
    own_out_ref[1] = r0[0]


def second_body(count_ref, r0, r1, r2, r3, own_ref, factor_ref, copies_ref, own_out_ref):
    refs = (r0, r1, r2, r3)
    tiles = arrived(count_ref[2], refs, 1) + arrived(count_ref[2], refs, 0)
    own = advanced(count_ref, own_ref.at[0], factor_ref, tiles)
    own_out_ref[...] = own
    for i in range(GROUP):
        copies_ref[i] = own


def third_body(count_ref, tiles_ref, own_ref, factor_ref, copies_ref, own_out_ref, packed_ref):
    tiles = [tiles_ref[i] for i in range((STEPS - 1) * TILES)]
    own = advanced(count_ref, own_ref, factor_ref, tiles)
    own_out_ref[...] = own
    for i in range(GROUP):
        copies_ref[i] = own
    for i, value in enumerate(tiles):
        packed_ref[i] = value


def middle_body(count_ref, *refs):
    sources = refs[:SOURCES]
    right_ref, panel_ref, inverses_ref = refs[SOURCES:SOURCES + 3]
    solved_ref, left_ref = refs[-2:]
    parts = []
    for step in range(STEPS - 1):
        solved = times_split(chosen(count_ref[1], sources, step * TILES), inverses_ref[step])
        solved_ref[:, step * WIDTH:(step + 1) * WIDTH] = solved
        parts.append(solved)
    solved = jnp.concatenate(parts, axis=1)
    for block in range(right_ref.shape[0]):
        product = times_split(solved, panel_ref[block, :, :(STEPS - 1) * WIDTH])
        left_ref[block] = right_ref[block] - product


def finish_body(count_ref, *refs):
    sources = refs[:SOURCES]
    own_ref, partly_ref, before_ref, panel_ref, inverses_ref = refs[SOURCES:SOURCES + 5]
    solved_ref, left_ref, sums_ref = refs[-3:]
    step = STEPS - 1
    solved = times_split(chosen(count_ref[1], sources, 0), inverses_ref[step])
    solved_ref[:, :step * WIDTH] = before_ref[...]
    solved_ref[:, step * WIDTH:] = solved
    for block in range(partly_ref.shape[0]):
        product = times_split(solved, panel_ref[block, :, step * WIDTH:])
        left = partly_ref[block] - product
        if block == 0:
            left = jnp.where(count_ref[0] >= 0, own_ref[...], left)
        left_ref[block] = left
        total = jnp.sum(left, axis=0, keepdims=True)
        square = jnp.sum(left * left, axis=0, keepdims=True)
        for i in range(8):
            sums_ref[i, 0, block:block + 1] = total
            sums_ref[i, 1, block:block + 1] = square


VMEM = pl.BlockSpec(memory_space=pltpu.VMEM)
SMEM = pl.BlockSpec(memory_space=pltpu.SMEM)


def shape(*dims):
    return jax.ShapeDtypeStruct(dims, f32)


def params(limit):
    return pltpu.CompilerParams(vmem_limit_bytes=limit << 20)


def cost(flops, size):
    return pl.CostEstimate(flops=flops, bytes_accessed=size, transcendentals=0)


def local(body, limit, outs, flops, size, *args):
    smem = [SMEM] if args[0].ndim == 1 else []
    return pl.pallas_call(
        body,
        out_shape=outs,
        in_specs=smem + [VMEM] * (len(args) - len(smem)),
        out_specs=[VMEM] * len(outs),
        compiler_params=params(limit),
        cost_estimate=cost(flops, size),
    )(*args)


def forward(value, step):
    ahead = (step + 1) * TILES
    return [
        lax.ppermute(
            value, ROWS, [(ahead - TILES + i, ahead + (i ^ change)) for i in range(TILES)]
        )
        for change in range(TILES)
    ]


def shards(factor_panel, right_side, inverses):
    blocks, _, rows, columns = factor_panel.shape
    members = right_side.shape[3]
    panel = factor_panel.reshape(blocks, rows, columns)
    right = right_side.reshape(blocks, rows, members).transpose(0, 2, 1)
    step_of = lax.axis_index(ROWS) // TILES
    lane = lax.axis_index("zl")
    count = jnp.stack([jnp.where(step_of < STEPS, step_of, -1), line_of(), lane])
    count = count.astype(jnp.int32)
    tile = shape(members, rows)
    group = shape(GROUP, members, rows)
    right, count = lax.optimization_barrier((right, count))

    own, = local(begin_body, 8, [tile], 1 << 34, 1 << 20, right)
    tiles = forward(own[None], 0)
    factor, = local(
        prepare_body, 16, [shape(rows, (STEPS - 1) * WIDTH)], 1 << 30, 4 << 20,
        panel, inverses,
    )
    own, = local(
        first_body, 8, [shape(2, members, rows)], 1 << 26, 1 << 20,
        count, *tiles, own, factor,
    )
    tiles = forward(own, 1)
    copies, own = local(second_body, 8, [group, tile], 1 << 27, 1 << 20, count, *tiles, own, factor)
    tiles = lax.all_to_all(copies, OWNERS, 0, 0)
    copies, own, packed = local(
        third_body, 8, [group, tile, shape(3 * TILES, members, rows)],
        1 << 27, 2 << 20, count, tiles, own, factor,
    )
    early = crossings(packed)
    received = lax.all_to_all(copies, OWNERS, 0, 0)
    ends = received[(STEPS - 1) * TILES:]
    late = crossings(ends)
    own, ends, *early = lax.optimization_barrier((own, ends, packed, *early))
    before, partly = local(
        middle_body, 16,
        [shape(members, (STEPS - 1) * WIDTH), shape(blocks, members, rows)],
        1 << 30, 12 << 20, count, *early, right, panel, inverses,
    )
    solved, left, sums = local(
        finish_body, 16,
        [shape(members, STEPS * WIDTH), shape(blocks, members, rows), shape(8, 2, blocks, rows)],
        1 << 28, 4 << 20, count, ends, *late, own, partly, before, panel, inverses,
    )
    sums = jnp.sum(lax.all_to_all(sums, MEM, 0, 0), axis=0)
    size = members * 8
    mean = sums[0] / size
    spread = sums[1] / size - mean * mean
    return (
        solved.T,
        left.transpose(0, 2, 1).reshape(right_side.shape),
        spread.reshape(blocks, 1, rows),
    )


def solution(mesh):
    fine = Mesh(mesh.devices.reshape(SIZES), AXES)
    return jax.shard_map(
        shards,
        mesh=fine,
        in_specs=(P(None, ROWS, None, None), P(None, ROWS, None, MEM), P()),
        out_specs=(P(None, MEM), P(None, ROWS, None, MEM), P(None, ROWS, None)),
        check_vma=False,
    )
```

```python
import jax
import jax.numpy as jnp
from jax import lax
from jax.experimental import pallas as pl
from jax.experimental.pallas import tpu as pltpu
from jax.sharding import Mesh, PartitionSpec as P

f32 = jnp.float32
bf16 = jnp.bfloat16
AXES = ("xh", "xl", "zh", "zl", "y", "core")
SIZES = (2, 2, 2, 4, 4, 2)
ROWS = AXES[:4]
OWNERS = AXES[1:4]
MEM = AXES[4:]
TILES = 4
STEPS = 4
WIDTH = 512
NT = (((1,), (1,)), ((), ()))
NN = (((1,), (0,)), ((), ()))
SOURCES = 2
GROUP = 16
ORDER = (2, 3, 1, 0)


def line_of():
    return lax.axis_index("xh")


def crossings(value):
    return [lax.ppermute(value, "xh", [(0, 1)])]


def split(value):
    high = value.astype(bf16)
    return high, (value - high.astype(f32)).astype(bf16)


def dot16(left, right, dims):
    return lax.dot_general(left, right, dims, preferred_element_type=f32)


def joined(ref, first):
    return jnp.concatenate([ref[first + i] for i in range(TILES)], axis=1)


def times_split(value, right):
    return times_halves(value, *split(right))


def times_halves(value, right_high, right_low):
    rows = value.shape[0]
    high, low = split(value)
    wide = dot16(jnp.concatenate([high, low], axis=0), right_high, NT)
    return wide[:rows] + wide[rows:] + dot16(high, right_low, NT)


def chosen(line, refs, first):
    value = joined(refs[0], first)
    for at, ref in enumerate(refs[1:]):
        value = jnp.where(line == at + 1, joined(ref, first), value)
    return value


def begin_body(right_ref, own_ref):
    own_ref[...] = right_ref[0]


def prepare_body(panel_ref, inverses_ref, high_ref, low_ref, part_ref, inverse_ref, sems):
    copies = []
    for step in range(STEPS - 1):
        columns = pl.ds(step * WIDTH, WIDTH)
        copies.append((
            pltpu.make_async_copy(
                panel_ref.at[0, :, columns], part_ref.at[step], sems.at[0, step]
            ),
            pltpu.make_async_copy(
                inverses_ref.at[step], inverse_ref.at[step], sems.at[1, step]
            ),
        ))
    for pair in copies:
        for copy in pair:
            copy.start()
    for step, pair in enumerate(copies):
        for copy in pair:
            copy.wait()
        factor = lax.dot_general(
            part_ref[step], inverse_ref[step], NN, precision=lax.Precision.HIGHEST,
            preferred_element_type=f32,
        )
        columns = slice(step * WIDTH, (step + 1) * WIDTH)
        high_ref[:, columns], low_ref[:, columns] = split(factor)


def prepare(panel, inverses):
    rows = panel.shape[1]
    number = STEPS - 1
    half = jax.ShapeDtypeStruct((rows, number * WIDTH), bf16)
    return pl.pallas_call(
        prepare_body,
        out_shape=[half, half],
        in_specs=[pl.BlockSpec(memory_space=pl.ANY)] * 2,
        out_specs=[VMEM] * 2,
        scratch_shapes=[
            pltpu.VMEM((number, rows, WIDTH), f32),
            pltpu.VMEM((number, WIDTH, WIDTH), f32),
            pltpu.SemaphoreType.DMA((2, number)),
        ],
        compiler_params=params(16),
        cost_estimate=cost(1 << 30, 4 << 20),
        name="prepare",
    )(panel, inverses)


def arrived(lane, refs, at):
    tiles = []
    for tile in range(TILES):
        wanted = jnp.bitwise_xor(lane, tile)
        value = refs[0][at]
        for change in range(1, TILES):
            value = jnp.where(wanted == change, refs[change][at], value)
        tiles.append(value)
    return tiles


def advanced(count_ref, own_ref, high_ref, low_ref, tiles):
    steps = len(tiles) // TILES
    change = times_halves(
        jnp.concatenate(tiles, axis=1), high_ref[:, :steps * WIDTH], low_ref[:, :steps * WIDTH]
    )
    return jnp.where(count_ref[0] == steps, own_ref[...] - change, own_ref[...])


def first_body(count_ref, r0, r1, r2, r3, own_ref, high_ref, low_ref, own_out_ref):
    own = advanced(count_ref, own_ref, high_ref, low_ref, arrived(count_ref[2], (r0, r1, r2, r3), 0))
    own_out_ref[0] = own
    own_out_ref[1] = r0[0]


def second_body(count_ref, r0, r1, r2, r3, own_ref, high_ref, low_ref, copies_ref, own_out_ref):
    refs = (r0, r1, r2, r3)
    tiles = arrived(count_ref[2], refs, 1) + arrived(count_ref[2], refs, 0)
    own = advanced(count_ref, own_ref.at[0], high_ref, low_ref, tiles)
    own_out_ref[...] = own
    for i in range(GROUP):
        copies_ref[i] = own


def third_body(count_ref, tiles_ref, own_ref, high_ref, low_ref, copies_ref, own_out_ref, packed_ref):
    tiles = [tiles_ref[i] for i in range((STEPS - 1) * TILES)]
    own = advanced(count_ref, own_ref, high_ref, low_ref, tiles)
    own_out_ref[...] = own
    for i in range(GROUP):
        copies_ref[i] = own
    for i, value in enumerate(tiles):
        packed_ref[i] = value


def middle_body(count_ref, *refs):
    sources = refs[:SOURCES]
    right_ref, panel_ref, inverses_ref = refs[SOURCES:SOURCES + 3]
    solved_ref, left_ref = refs[-2:]
    parts = []
    for step in range(STEPS - 1):
        solved = times_split(chosen(count_ref[1], sources, step * TILES), inverses_ref[step])
        solved_ref[:, step * WIDTH:(step + 1) * WIDTH] = solved
        parts.append(solved)
    solved = jnp.concatenate(parts, axis=1)
    for block in range(right_ref.shape[0]):
        product = times_split(solved, panel_ref[block, :, :(STEPS - 1) * WIDTH])
        left_ref[block] = right_ref[block] - product


def finish_body(count_ref, *refs):
    sources = refs[:SOURCES]
    own_ref, partly_ref, before_ref, panel_ref, inverses_ref = refs[SOURCES:SOURCES + 5]
    solved_ref, left_ref, sums_ref = refs[-3:]
    step = STEPS - 1
    solved = times_split(chosen(count_ref[1], sources, 0), inverses_ref[step])
    solved_ref[:, :step * WIDTH] = before_ref[...]
    solved_ref[:, step * WIDTH:] = solved
    for block in range(partly_ref.shape[0]):
        product = times_split(solved, panel_ref[block, :, step * WIDTH:])
        left = partly_ref[block] - product
        if block == 0:
            left = jnp.where(count_ref[0] >= 0, own_ref[...], left)
        left_ref[block] = left
        total = jnp.sum(left, axis=0, keepdims=True)
        square = jnp.sum(left * left, axis=0, keepdims=True)
        for i in range(8):
            sums_ref[i, 0, block:block + 1] = total
            sums_ref[i, 1, block:block + 1] = square


VMEM = pl.BlockSpec(memory_space=pltpu.VMEM)
SMEM = pl.BlockSpec(memory_space=pltpu.SMEM)


def shape(*dims):
    return jax.ShapeDtypeStruct(dims, f32)


def params(limit):
    return pltpu.CompilerParams(vmem_limit_bytes=limit << 20)


def cost(flops, size):
    return pl.CostEstimate(flops=flops, bytes_accessed=size, transcendentals=0)


def local(body, limit, outs, flops, size, *args):
    smem = [SMEM] if args[0].ndim == 1 else []
    return pl.pallas_call(
        body,
        out_shape=outs,
        in_specs=smem + [VMEM] * (len(args) - len(smem)),
        out_specs=[VMEM] * len(outs),
        compiler_params=params(limit),
        cost_estimate=cost(flops, size),
    )(*args)


def forward(value, step):
    ahead = (step + 1) * TILES
    pieces = {
        change: lax.ppermute(
            value, ROWS, [(ahead - TILES + i, ahead + (i ^ change)) for i in range(TILES)]
        )
        for change in ORDER
    }
    return [pieces[change] for change in range(TILES)]


def shards(factor_panel, right_side, inverses):
    blocks, _, rows, columns = factor_panel.shape
    members = right_side.shape[3]
    panel = factor_panel.reshape(blocks, rows, columns)
    right = right_side.reshape(blocks, rows, members).transpose(0, 2, 1)
    step_of = lax.axis_index(ROWS) // TILES
    lane = lax.axis_index("zl")
    count = jnp.stack([jnp.where(step_of < STEPS, step_of, -1), line_of(), lane])
    count = count.astype(jnp.int32)
    tile = shape(members, rows)
    group = shape(GROUP, members, rows)
    right, count = lax.optimization_barrier((right, count))

    own, = local(begin_body, 8, [tile], 1 << 20, 1 << 20, right)
    tiles = forward(own[None], 0)
    factor = prepare(panel, inverses)
    own, = local(
        first_body, 8, [shape(2, members, rows)], 1 << 34, 1 << 20,
        count, *tiles, own, *factor,
    )
    tiles = forward(own, 1)
    copies, own = local(
        second_body, 8, [group, tile], 1 << 27, 1 << 20, count, *tiles, own, *factor,
    )
    tiles = lax.all_to_all(copies, OWNERS, 0, 0)
    copies, own, packed = local(
        third_body, 8, [group, tile, shape(3 * TILES, members, rows)],
        1 << 27, 2 << 20, count, tiles, own, *factor,
    )
    early = crossings(packed)
    received = lax.all_to_all(copies, OWNERS, 0, 0)
    ends = received[(STEPS - 1) * TILES:]
    late = crossings(ends)
    own, ends, *early = lax.optimization_barrier((own, ends, packed, *early))
    before, partly = local(
        middle_body, 16,
        [shape(members, (STEPS - 1) * WIDTH), shape(blocks, members, rows)],
        1 << 30, 12 << 20, count, *early, right, panel, inverses,
    )
    solved, left, sums = local(
        finish_body, 16,
        [shape(members, STEPS * WIDTH), shape(blocks, members, rows), shape(8, 2, blocks, rows)],
        1 << 28, 4 << 20, count, ends, *late, own, partly, before, panel, inverses,
    )
    sums = jnp.sum(lax.all_to_all(sums, MEM, 0, 0), axis=0)
    size = members * 8
    mean = sums[0] / size
    spread = sums[1] / size - mean * mean
    return (
        solved.T,
        left.transpose(0, 2, 1).reshape(right_side.shape),
        spread.reshape(blocks, 1, rows),
    )


def solution(mesh):
    fine = Mesh(mesh.devices.reshape(SIZES), AXES)
    return jax.shard_map(
        shards,
        mesh=fine,
        in_specs=(P(None, ROWS, None, None), P(None, ROWS, None, MEM), P()),
        out_specs=(P(None, MEM), P(None, ROWS, None, MEM), P(None, ROWS, None)),
        check_vma=False,
    )
```

```python
import jax
import jax.numpy as jnp
from jax import lax
from jax.experimental import pallas as pl
from jax.experimental.pallas import tpu as pltpu
from jax.sharding import Mesh, PartitionSpec as P

f32 = jnp.float32
bf16 = jnp.bfloat16
AXES = ("xh", "xl", "zh", "zl", "y", "core")
SIZES = (2, 2, 2, 4, 4, 2)
ROWS = AXES[:4]
OWNERS = AXES[1:4]
MEM = AXES[4:]
TILES = 4
STEPS = 4
WIDTH = 512
NT = (((1,), (1,)), ((), ()))
NN = (((1,), (0,)), ((), ()))
SOURCES = 2
GROUP = 16
ORDER = (2, 3, 1, 0)


def line_of():
    return lax.axis_index("xh")


def crossings(value):
    return [lax.ppermute(value, ROWS[:2], [(0, 3), (1, 2)])]


def split(value):
    high = value.astype(bf16)
    return high, (value - high.astype(f32)).astype(bf16)


def dot16(left, right, dims):
    return lax.dot_general(left, right, dims, preferred_element_type=f32)


def joined(ref, first):
    return jnp.concatenate([ref[first + i] for i in range(TILES)], axis=1)


def times_split(value, right):
    return times_halves(value, *split(right))


def times_halves(value, right_high, right_low):
    rows = value.shape[0]
    high, low = split(value)
    wide = dot16(jnp.concatenate([high, low], axis=0), right_high, NT)
    return wide[:rows] + wide[rows:] + dot16(high, right_low, NT)


def chosen(line, refs, first):
    value = joined(refs[0], first)
    for at, ref in enumerate(refs[1:]):
        value = jnp.where(line == at + 1, joined(ref, first), value)
    return value


def begin_body(right_ref, own_ref):
    own_ref[...] = right_ref[0]


def prepare_body(panel_ref, inverses_ref, high_ref, low_ref, part_ref, inverse_ref, sems):
    copies = []
    for step in range(STEPS - 1):
        columns = pl.ds(step * WIDTH, WIDTH)
        copies.append((
            pltpu.make_async_copy(
                panel_ref.at[0, :, columns], part_ref.at[step], sems.at[0, step]
            ),
            pltpu.make_async_copy(
                inverses_ref.at[step], inverse_ref.at[step], sems.at[1, step]
            ),
        ))
    for pair in copies:
        for copy in pair:
            copy.start()
    for step, pair in enumerate(copies):
        for copy in pair:
            copy.wait()
        high, low = split(part_ref[step])
        inverse_high, inverse_low = split(inverse_ref[step])
        wide = dot16(jnp.concatenate([high, low], axis=0), inverse_high, NN)
        rows = high.shape[0]
        factor = wide[:rows] + wide[rows:] + dot16(high, inverse_low, NN)
        columns = slice(step * WIDTH, (step + 1) * WIDTH)
        high_ref[:, columns], low_ref[:, columns] = split(factor)


def prepare(panel, inverses):
    rows = panel.shape[1]
    number = STEPS - 1
    half = jax.ShapeDtypeStruct((rows, number * WIDTH), bf16)
    return pl.pallas_call(
        prepare_body,
        out_shape=[half, half],
        in_specs=[pl.BlockSpec(memory_space=pl.ANY)] * 2,
        out_specs=[VMEM] * 2,
        scratch_shapes=[
            pltpu.VMEM((number, rows, WIDTH), f32),
            pltpu.VMEM((number, WIDTH, WIDTH), f32),
            pltpu.SemaphoreType.DMA((2, number)),
        ],
        compiler_params=params(16),
        cost_estimate=cost(1 << 30, 4 << 20),
        name="prepare",
    )(panel, inverses)


def arrived(lane, refs, at):
    tiles = []
    for tile in range(TILES):
        wanted = jnp.bitwise_xor(lane, tile)
        value = refs[0][at]
        for change, ref in zip(ORDER[1:], refs[1:]):
            value = jnp.where(wanted == change, ref[at], value)
        tiles.append(value)
    return tiles


def advanced(count_ref, own_ref, high_ref, low_ref, tiles):
    steps = len(tiles) // TILES
    change = times_halves(
        jnp.concatenate(tiles, axis=1), high_ref[:, :steps * WIDTH], low_ref[:, :steps * WIDTH]
    )
    return jnp.where(count_ref[0] == steps, own_ref[...] - change, own_ref[...])


def first_body(count_ref, r0, r1, r2, r3, own_ref, high_ref, low_ref, own_out_ref):
    own = advanced(count_ref, own_ref, high_ref, low_ref, arrived(count_ref[2], (r0, r1, r2, r3), 0))
    own_out_ref[0] = own
    own_out_ref[1] = r3[0]


def second_body(count_ref, r0, r1, r2, r3, own_ref, high_ref, low_ref, copies_ref, own_out_ref):
    refs = (r0, r1, r2, r3)
    tiles = arrived(count_ref[2], refs, 1) + arrived(count_ref[2], refs, 0)
    own = advanced(count_ref, own_ref.at[0], high_ref, low_ref, tiles)
    own_out_ref[...] = own
    for i in range(GROUP):
        copies_ref[i] = own


def third_body(count_ref, tiles_ref, own_ref, high_ref, low_ref, copies_ref, own_out_ref, packed_ref):
    tiles = [tiles_ref[i] for i in range((STEPS - 1) * TILES)]
    own = advanced(count_ref, own_ref, high_ref, low_ref, tiles)
    own_out_ref[...] = own
    for i in range(GROUP):
        copies_ref[i] = own
    for i, value in enumerate(tiles):
        packed_ref[i] = value


def middle_body(count_ref, *refs):
    sources = refs[:SOURCES]
    right_ref, panel_ref, inverses_ref = refs[SOURCES:SOURCES + 3]
    solved_ref, left_ref = refs[-2:]
    parts = []
    for step in range(STEPS - 1):
        solved = times_split(chosen(count_ref[1], sources, step * TILES), inverses_ref[step])
        solved_ref[:, step * WIDTH:(step + 1) * WIDTH] = solved
        parts.append(solved)
    solved = jnp.concatenate(parts, axis=1)
    for block in range(right_ref.shape[0]):
        product = times_split(solved, panel_ref[block, :, :(STEPS - 1) * WIDTH])
        left_ref[block] = right_ref[block] - product


def finish_body(count_ref, *refs):
    sources = refs[:SOURCES]
    own_ref, partly_ref, before_ref, panel_ref, inverses_ref = refs[SOURCES:SOURCES + 5]
    solved_ref, left_ref, sums_ref = refs[-3:]
    step = STEPS - 1
    solved = times_split(chosen(count_ref[1], sources, 0), inverses_ref[step])
    solved_ref[:, :step * WIDTH] = before_ref[...]
    solved_ref[:, step * WIDTH:] = solved
    for block in range(partly_ref.shape[0]):
        product = times_split(solved, panel_ref[block, :, step * WIDTH:])
        left = partly_ref[block] - product
        if block == 0:
            left = jnp.where(count_ref[0] >= 0, own_ref[...], left)
        left_ref[block] = left
        total = jnp.sum(left, axis=0, keepdims=True)
        square = jnp.sum(left * left, axis=0, keepdims=True)
        for i in range(8):
            sums_ref[i, 0, block:block + 1] = total
            sums_ref[i, 1, block:block + 1] = square


VMEM = pl.BlockSpec(memory_space=pltpu.VMEM)
SMEM = pl.BlockSpec(memory_space=pltpu.SMEM)


def shape(*dims):
    return jax.ShapeDtypeStruct(dims, f32)


def params(limit):
    return pltpu.CompilerParams(vmem_limit_bytes=limit << 20)


def cost(flops, size):
    return pl.CostEstimate(flops=flops, bytes_accessed=size, transcendentals=0)


def local(body, limit, outs, flops, size, *args):
    smem = [SMEM] if args[0].ndim == 1 else []
    return pl.pallas_call(
        body,
        out_shape=outs,
        in_specs=smem + [VMEM] * (len(args) - len(smem)),
        out_specs=[VMEM] * len(outs),
        compiler_params=params(limit),
        cost_estimate=cost(flops, size),
    )(*args)


def forward(value, step):
    ahead = (step + 1) * TILES
    return [
        lax.ppermute(
            value, ROWS, [(ahead - TILES + i, ahead + (i ^ change)) for i in range(TILES)]
        )
        for change in ORDER
    ]


def shards(factor_panel, right_side, inverses):
    blocks, _, rows, columns = factor_panel.shape
    members = right_side.shape[3]
    panel = factor_panel.reshape(blocks, rows, columns)
    right = right_side.reshape(blocks, rows, members).transpose(0, 2, 1)
    step_of = lax.axis_index(ROWS) // TILES
    lane = lax.axis_index("zl")
    count = jnp.stack([jnp.where(step_of < STEPS, step_of, -1), line_of(), lane])
    count = count.astype(jnp.int32)
    tile = shape(members, rows)
    group = shape(GROUP, members, rows)
    right, count = lax.optimization_barrier((right, count))

    own, = local(begin_body, 8, [tile], 1 << 20, 1 << 20, right)
    tiles = forward(own[None], 0)
    factor = prepare(panel, inverses)
    own, = local(
        first_body, 8, [shape(2, members, rows)], 1 << 34, 1 << 20,
        count, *tiles, own, *factor,
    )
    tiles = forward(own, 1)
    copies, own = local(
        second_body, 8, [group, tile], 1 << 27, 1 << 20, count, *tiles, own, *factor,
    )
    tiles = lax.all_to_all(copies, OWNERS, 0, 0)
    copies, own, packed = local(
        third_body, 8, [group, tile, shape(3 * TILES, members, rows)],
        1 << 27, 2 << 20, count, tiles, own, *factor,
    )
    early = crossings(packed)
    received = lax.all_to_all(copies, OWNERS, 0, 0)
    ends = received[(STEPS - 1) * TILES:]
    late = crossings(ends)
    own, ends, *early = lax.optimization_barrier((own, ends, packed, *early))
    before, partly = local(
        middle_body, 16,
        [shape(members, (STEPS - 1) * WIDTH), shape(blocks, members, rows)],
        1 << 30, 12 << 20, count, *early, right, panel, inverses,
    )
    solved, left, sums = local(
        finish_body, 16,
        [shape(members, STEPS * WIDTH), shape(blocks, members, rows), shape(8, 2, blocks, rows)],
        1 << 28, 4 << 20, count, ends, *late, own, partly, before, panel, inverses,
    )
    sums = jnp.sum(lax.all_to_all(sums, MEM, 0, 0), axis=0)
    size = members * 8
    mean = sums[0] / size
    spread = sums[1] / size - mean * mean
    return (
        solved.T,
        left.transpose(0, 2, 1).reshape(right_side.shape),
        spread.reshape(blocks, 1, rows),
    )


def solution(mesh):
    fine = Mesh(mesh.devices.reshape(SIZES), AXES)
    return jax.shard_map(
        shards,
        mesh=fine,
        in_specs=(P(None, ROWS, None, None), P(None, ROWS, None, MEM), P()),
        out_specs=(P(None, MEM), P(None, ROWS, None, MEM), P(None, ROWS, None)),
        check_vma=False,
    )
```

```python
import jax
import jax.numpy as jnp
from jax import lax
from jax.experimental import pallas as pl
from jax.experimental.pallas import tpu as pltpu
from jax.sharding import Mesh, PartitionSpec as P

f32 = jnp.float32
bf16 = jnp.bfloat16
AXES = ("xh", "xl", "zh", "zl", "y", "core")
SIZES = (2, 2, 2, 4, 4, 2)
ROWS = AXES[:4]
OWNERS = AXES[1:4]
MEM = AXES[4:]
TILES = 4
STEPS = 4
WIDTH = 512
NT = (((1,), (1,)), ((), ()))
NN = (((1,), (0,)), ((), ()))
SOURCES = 2
GROUP = 16
ORDER = (2, 3, 1, 0)


def line_of():
    return lax.axis_index("xh")


EARLY = [(0, 2), (1, 3)]
LATE = [(0, 3), (1, 2)]


def crossings(value, pairs):
    return [lax.ppermute(value, ROWS[:2], pairs)]


def split(value):
    high = value.astype(bf16)
    return high, (value - high.astype(f32)).astype(bf16)


def dot16(left, right, dims):
    return lax.dot_general(left, right, dims, preferred_element_type=f32)


def joined(ref, first):
    return jnp.concatenate([ref[first + i] for i in range(TILES)], axis=1)


def times_split(value, right):
    return times_halves(value, *split(right))


def times_halves(value, right_high, right_low):
    rows = value.shape[0]
    high, low = split(value)
    wide = dot16(jnp.concatenate([high, low], axis=0), right_high, NT)
    return wide[:rows] + wide[rows:] + dot16(high, right_low, NT)


def chosen(line, refs, first):
    value = joined(refs[0], first)
    for at, ref in enumerate(refs[1:]):
        value = jnp.where(line == at + 1, joined(ref, first), value)
    return value


def begin_body(right_ref, own_ref):
    own_ref[...] = right_ref[0]


def prepare_body(panel_ref, inverses_ref, high_ref, low_ref, part_ref, inverse_ref, sems):
    copies = []
    for step in range(STEPS - 1):
        columns = pl.ds(step * WIDTH, WIDTH)
        copies.append((
            pltpu.make_async_copy(
                panel_ref.at[0, :, columns], part_ref.at[step], sems.at[0, step]
            ),
            pltpu.make_async_copy(
                inverses_ref.at[step], inverse_ref.at[step], sems.at[1, step]
            ),
        ))
    for pair in copies:
        for copy in pair:
            copy.start()
    for step, pair in enumerate(copies):
        for copy in pair:
            copy.wait()
        high, low = split(part_ref[step])
        inverse_high, inverse_low = split(inverse_ref[step])
        wide = dot16(jnp.concatenate([high, low], axis=0), inverse_high, NN)
        rows = high.shape[0]
        factor = wide[:rows] + wide[rows:] + dot16(high, inverse_low, NN)
        columns = slice(step * WIDTH, (step + 1) * WIDTH)
        high_ref[:, columns], low_ref[:, columns] = split(factor)


def prepare(panel, inverses):
    rows = panel.shape[1]
    number = STEPS - 1
    half = jax.ShapeDtypeStruct((rows, number * WIDTH), bf16)
    return pl.pallas_call(
        prepare_body,
        out_shape=[half, half],
        in_specs=[pl.BlockSpec(memory_space=pl.ANY)] * 2,
        out_specs=[VMEM] * 2,
        scratch_shapes=[
            pltpu.VMEM((number, rows, WIDTH), f32),
            pltpu.VMEM((number, WIDTH, WIDTH), f32),
            pltpu.SemaphoreType.DMA((2, number)),
        ],
        compiler_params=params(16),
        cost_estimate=cost(1 << 30, 4 << 20),
        name="prepare",
    )(panel, inverses)


def arrived(lane, refs, at):
    tiles = []
    for tile in range(TILES):
        wanted = jnp.bitwise_xor(lane, tile)
        value = refs[0][at]
        for change, ref in zip(ORDER[1:], refs[1:]):
            value = jnp.where(wanted == change, ref[at], value)
        tiles.append(value)
    return tiles


def advanced(count_ref, own_ref, high_ref, low_ref, tiles):
    steps = len(tiles) // TILES
    change = times_halves(
        jnp.concatenate(tiles, axis=1), high_ref[:, :steps * WIDTH], low_ref[:, :steps * WIDTH]
    )
    return jnp.where(count_ref[0] == steps, own_ref[...] - change, own_ref[...])


def first_body(count_ref, r0, r1, r2, r3, own_ref, high_ref, low_ref, own_out_ref):
    own = advanced(count_ref, own_ref, high_ref, low_ref, arrived(count_ref[2], (r0, r1, r2, r3), 0))
    own_out_ref[0] = own
    own_out_ref[1] = r3[0]


def second_body(count_ref, r0, r1, r2, r3, own_ref, high_ref, low_ref, copies_ref, own_out_ref):
    refs = (r0, r1, r2, r3)
    tiles = arrived(count_ref[2], refs, 1) + arrived(count_ref[2], refs, 0)
    own = advanced(count_ref, own_ref.at[0], high_ref, low_ref, tiles)
    own_out_ref[...] = own
    for i in range(GROUP):
        copies_ref[i] = own


def third_body(count_ref, tiles_ref, own_ref, high_ref, low_ref, copies_ref, own_out_ref, packed_ref):
    tiles = [tiles_ref[i] for i in range((STEPS - 1) * TILES)]
    own = advanced(count_ref, own_ref, high_ref, low_ref, tiles)
    own_out_ref[...] = own
    for i in range(GROUP):
        copies_ref[i] = own
    for i, value in enumerate(tiles):
        packed_ref[i] = value


def middle_body(count_ref, *refs):
    sources = refs[:SOURCES]
    right_ref, panel_ref, inverses_ref = refs[SOURCES:SOURCES + 3]
    solved_ref, left_ref = refs[-2:]
    parts = []
    for step in range(STEPS - 1):
        solved = times_split(chosen(count_ref[1], sources, step * TILES), inverses_ref[step])
        solved_ref[:, step * WIDTH:(step + 1) * WIDTH] = solved
        parts.append(solved)
    solved = jnp.concatenate(parts, axis=1)
    for block in range(right_ref.shape[0]):
        product = times_split(solved, panel_ref[block, :, :(STEPS - 1) * WIDTH])
        left_ref[block] = right_ref[block] - product


def finish_body(count_ref, *refs):
    sources = refs[:SOURCES]
    own_ref, partly_ref, panel_ref, inverses_ref = refs[SOURCES:SOURCES + 4]
    solved_ref, low_ref, high_ref, sums_ref = refs[-4:]
    step = STEPS - 1
    solved = times_split(chosen(count_ref[1], sources, 0), inverses_ref[step])
    solved_ref[...] = solved
    for block in range(partly_ref.shape[0]):
        product = times_split(solved, panel_ref[block, :, step * WIDTH:])
        left = partly_ref[block] - product
        if block == 0:
            left = jnp.where(count_ref[0] >= 0, own_ref[...], left)
        half = low_ref if 2 * block < partly_ref.shape[0] else high_ref
        half[block % half.shape[0]] = left
        sums_ref[0, block:block + 1] = jnp.sum(left, axis=0, keepdims=True)
        sums_ref[1, block:block + 1] = jnp.sum(left * left, axis=0, keepdims=True)


VMEM = pl.BlockSpec(memory_space=pltpu.VMEM)
SMEM = pl.BlockSpec(memory_space=pltpu.SMEM)


def shape(*dims):
    return jax.ShapeDtypeStruct(dims, f32)


def params(limit):
    return pltpu.CompilerParams(vmem_limit_bytes=limit << 20)


def cost(flops, size):
    return pl.CostEstimate(flops=flops, bytes_accessed=size, transcendentals=0)


def local(body, limit, outs, flops, size, *args):
    smem = [SMEM] if args[0].ndim == 1 else []
    return pl.pallas_call(
        body,
        out_shape=outs,
        in_specs=smem + [VMEM] * (len(args) - len(smem)),
        out_specs=[VMEM] * len(outs),
        compiler_params=params(limit),
        cost_estimate=cost(flops, size),
    )(*args)


def forward(value, step):
    ahead = (step + 1) * TILES
    pieces = []
    for change in ORDER:
        pieces.append(lax.ppermute(
            value, ROWS, [(ahead - TILES + i, ahead + (i ^ change)) for i in range(TILES)]
        ))
    return pieces


def shards(factor_panel, right_side, inverses):
    blocks, _, rows, columns = factor_panel.shape
    members = right_side.shape[3]
    panel = factor_panel.reshape(blocks, rows, columns)
    right = right_side.reshape(blocks, rows, members).transpose(0, 2, 1)
    step_of = lax.axis_index(ROWS) // TILES
    lane = lax.axis_index("zl")
    count = jnp.stack([jnp.where(step_of < STEPS, step_of, -1), line_of(), lane])
    count = count.astype(jnp.int32)
    tile = shape(members, rows)
    group = shape(GROUP, members, rows)
    right, count = lax.optimization_barrier((right, count))

    own, = local(begin_body, 8, [tile], 1 << 20, 1 << 20, right)
    tiles = forward(own[None], 0)
    factor = prepare(panel, inverses)
    own, = local(
        first_body, 8, [shape(2, members, rows)], 1 << 34, 1 << 20,
        count, *tiles, own, *factor,
    )
    tiles = forward(own, 1)
    copies, own = local(
        second_body, 8, [group, tile], 1 << 27, 1 << 20, count, *tiles, own, *factor,
    )
    tiles = lax.all_to_all(copies, OWNERS, 0, 0)
    copies, own, packed = local(
        third_body, 8, [group, tile, shape(3 * TILES, members, rows)],
        1 << 27, 2 << 20, count, tiles, own, *factor,
    )
    early = crossings(packed, EARLY)
    received = lax.all_to_all(copies, OWNERS, 0, 0)
    ends = received[(STEPS - 1) * TILES:]
    late = crossings(ends, LATE)
    own, ends, *early = lax.optimization_barrier((own, ends, packed, *early))
    before, partly = local(
        middle_body, 16,
        [shape(members, (STEPS - 1) * WIDTH), shape(blocks, members, rows)],
        1 << 30, 12 << 20, count, *early, right, panel, inverses,
    )
    last, low, high, sums = local(
        finish_body, 16,
        [shape(members, WIDTH)] + [shape(blocks // 2, members, rows)] * 2 + [shape(2, blocks, rows)],
        1 << 28, 4 << 20, count, ends, *late, own, partly, panel, inverses,
    )
    sums = sums + lax.ppermute(sums, "core", [(0, 1), (1, 0)])
    others = [
        lax.ppermute(sums, "y", [(i, i ^ change) for i in range(4)]) for change in (1, 2, 3)
    ]
    sums = sums + others[0] + (others[1] + others[2])
    solved = jnp.concatenate([before, last], axis=1)
    left = jnp.concatenate([low, high], axis=0)
    size = members * 8
    mean = sums[0] / size
    spread = sums[1] / size - mean * mean
    return (
        solved.T,
        left.transpose(0, 2, 1).reshape(right_side.shape),
        spread.reshape(blocks, 1, rows),
    )


def solution(mesh):
    fine = Mesh(mesh.devices.reshape(SIZES), AXES)
    return jax.shard_map(
        shards,
        mesh=fine,
        in_specs=(P(None, ROWS, None, None), P(None, ROWS, None, MEM), P()),
        out_specs=(P(None, MEM), P(None, ROWS, None, MEM), P(None, ROWS, None)),
        check_vma=False,
    )
```

```python
import jax
import jax.numpy as jnp
from jax import lax
from jax.experimental import pallas as pl
from jax.experimental.pallas import tpu as pltpu
from jax.sharding import Mesh, PartitionSpec as P

f32 = jnp.float32
bf16 = jnp.bfloat16
AXES = ("xh", "xl", "zh", "zl", "y", "core")
SIZES = (2, 2, 2, 4, 4, 2)
ROWS = AXES[:4]
OWNERS = AXES[1:4]
MEM = AXES[4:]
TILES = 4
STEPS = 4
WIDTH = 512
NT = (((1,), (1,)), ((), ()))
NN = (((1,), (0,)), ((), ()))
SOURCES = 2
GROUP = 16
ORDER = (2, 3, 1, 0)


def line_of():
    return lax.axis_index("xh")


def step_of():
    return lax.axis_index("xh") * 4 + lax.axis_index("xl") * 2 + lax.axis_index("zh")


EARLY = [(0, 2), (1, 3)]
LATE = [(0, 3), (1, 2)]


def crossings(value, pairs):
    return [lax.ppermute(value, ROWS[:2], pairs)]


def split(value):
    high = value.astype(bf16)
    return high, (value - high.astype(f32)).astype(bf16)


def dot16(left, right, dims):
    return lax.dot_general(left, right, dims, preferred_element_type=f32)


def joined(ref, first):
    return jnp.concatenate([ref[first + i] for i in range(TILES)], axis=1)


def times_split(value, right):
    return times_halves(value, *split(right))


def times_halves(value, right_high, right_low):
    rows = value.shape[0]
    high, low = split(value)
    wide = dot16(jnp.concatenate([high, low], axis=0), right_high, NT)
    return wide[:rows] + wide[rows:] + dot16(high, right_low, NT)


def chosen(line, refs, first):
    value = joined(refs[0], first)
    for at, ref in enumerate(refs[1:]):
        value = jnp.where(line == at + 1, joined(ref, first), value)
    return value


def begin_body(right_ref, own_ref):
    own_ref[...] = right_ref[0]


def prepare_body(panel_ref, inverses_ref, high_ref, low_ref, part_ref, inverse_ref, sems):
    copies = []
    for step in range(STEPS - 1):
        columns = pl.ds(step * WIDTH, WIDTH)
        copies.append((
            pltpu.make_async_copy(
                panel_ref.at[0, :, columns], part_ref.at[step], sems.at[0, step]
            ),
            pltpu.make_async_copy(
                inverses_ref.at[step], inverse_ref.at[step], sems.at[1, step]
            ),
        ))
    for pair in copies:
        for copy in pair:
            copy.start()
    for step, pair in enumerate(copies):
        for copy in pair:
            copy.wait()
        high, low = split(part_ref[step])
        inverse_high, inverse_low = split(inverse_ref[step])
        wide = dot16(jnp.concatenate([high, low], axis=0), inverse_high, NN)
        rows = high.shape[0]
        factor = wide[:rows] + wide[rows:] + dot16(high, inverse_low, NN)
        columns = slice(step * WIDTH, (step + 1) * WIDTH)
        high_ref[:, columns], low_ref[:, columns] = split(factor)


def prepare(panel, inverses):
    rows = panel.shape[1]
    number = STEPS - 1
    half = jax.ShapeDtypeStruct((rows, number * WIDTH), bf16)
    return pl.pallas_call(
        prepare_body,
        out_shape=[half, half],
        in_specs=[pl.BlockSpec(memory_space=pl.ANY)] * 2,
        out_specs=[VMEM] * 2,
        scratch_shapes=[
            pltpu.VMEM((number, rows, WIDTH), f32),
            pltpu.VMEM((number, WIDTH, WIDTH), f32),
            pltpu.SemaphoreType.DMA((2, number)),
        ],
        compiler_params=params(16),
        cost_estimate=cost(1 << 30, 4 << 20),
        name="prepare",
    )(panel, inverses)


def arrived(lane, refs, at):
    tiles = []
    for tile in range(TILES):
        wanted = jnp.bitwise_xor(lane, tile)
        value = refs[0][at]
        for change, ref in zip(ORDER[1:], refs[1:]):
            value = jnp.where(wanted == change, ref[at], value)
        tiles.append(value)
    return tiles


def advanced(own_ref, high_ref, low_ref, tiles):
    steps = len(tiles) // TILES
    change = times_halves(
        jnp.concatenate(tiles, axis=1), high_ref[:, :steps * WIDTH], low_ref[:, :steps * WIDTH]
    )
    return jnp.where(step_of() == steps, own_ref[...] - change, own_ref[...])


def first_body(r0, r1, r2, r3, own_ref, high_ref, low_ref, own_out_ref):
    own = advanced(own_ref, high_ref, low_ref, arrived(lax.axis_index("zl"), (r0, r1, r2, r3), 0))
    own_out_ref[0] = own
    own_out_ref[1] = r3[0]


def second_body(r0, r1, r2, r3, own_ref, high_ref, low_ref, copies_ref, own_out_ref):
    refs = (r0, r1, r2, r3)
    tiles = arrived(lax.axis_index("zl"), refs, 1) + arrived(lax.axis_index("zl"), refs, 0)
    own = advanced(own_ref.at[0], high_ref, low_ref, tiles)
    own_out_ref[...] = own
    for i in range(GROUP):
        copies_ref[i] = own


def third_body(tiles_ref, own_ref, high_ref, low_ref, copies_ref, own_out_ref, packed_ref):
    tiles = [tiles_ref[i] for i in range((STEPS - 1) * TILES)]
    own = advanced(own_ref, high_ref, low_ref, tiles)
    own_out_ref[...] = own
    for i in range(GROUP):
        copies_ref[i] = own
    for i, value in enumerate(tiles):
        packed_ref[i] = value


def middle_body(*refs):
    sources = refs[:SOURCES]
    right_ref, panel_ref, inverses_ref = refs[SOURCES:SOURCES + 3]
    solved_ref, left_ref = refs[-2:]
    parts = []
    for step in range(STEPS - 1):
        solved = times_split(chosen(line_of(), sources, step * TILES), inverses_ref[step])
        solved_ref[:, step * WIDTH:(step + 1) * WIDTH] = solved
        parts.append(solved)
    solved = jnp.concatenate(parts, axis=1)
    for block in range(right_ref.shape[0]):
        product = times_split(solved, panel_ref[block, :, :(STEPS - 1) * WIDTH])
        left_ref[block] = right_ref[block] - product


def finish_body(*refs):
    sources = refs[:SOURCES]
    own_ref, partly_ref, panel_ref, inverses_ref = refs[SOURCES:SOURCES + 4]
    solved_ref, low_ref, high_ref, sums_ref = refs[-4:]
    step = STEPS - 1
    solved = times_split(chosen(line_of(), sources, 0), inverses_ref[step])
    solved_ref[...] = solved
    for block in range(partly_ref.shape[0]):
        product = times_split(solved, panel_ref[block, :, step * WIDTH:])
        left = partly_ref[block] - product
        if block == 0:
            left = jnp.where(step_of() < STEPS, own_ref[...], left)
        half = low_ref if 2 * block < partly_ref.shape[0] else high_ref
        half[block % half.shape[0]] = left
        sums_ref[0, block:block + 1] = jnp.sum(left, axis=0, keepdims=True)
        sums_ref[1, block:block + 1] = jnp.sum(left * left, axis=0, keepdims=True)


VMEM = pl.BlockSpec(memory_space=pltpu.VMEM)


def shape(*dims):
    return jax.ShapeDtypeStruct(dims, f32)


def params(limit):
    return pltpu.CompilerParams(vmem_limit_bytes=limit << 20)


def cost(flops, size):
    return pl.CostEstimate(flops=flops, bytes_accessed=size, transcendentals=0)


def local(body, limit, outs, flops, size, *args):
    return pl.pallas_call(
        body,
        out_shape=outs,
        in_specs=[VMEM] * len(args),
        out_specs=[VMEM] * len(outs),
        compiler_params=params(limit),
        cost_estimate=cost(flops, size),
    )(*args)


def forward(value, step):
    ahead = (step + 1) * TILES
    pieces = []
    for change in ORDER:
        pieces.append(lax.ppermute(
            value, ROWS, [(ahead - TILES + i, ahead + (i ^ change)) for i in range(TILES)]
        ))
    return pieces


def shards(factor_panel, right_side, inverses):
    blocks, _, rows, columns = factor_panel.shape
    members = right_side.shape[3]
    panel = factor_panel.reshape(blocks, rows, columns)
    right = right_side.reshape(blocks, rows, members).transpose(0, 2, 1)
    tile = shape(members, rows)
    group = shape(GROUP, members, rows)

    own, = local(begin_body, 8, [tile], 1 << 20, 1 << 20, right)
    tiles = forward(own[None], 0)
    factor = prepare(panel, inverses)
    own, = local(
        first_body, 8, [shape(2, members, rows)], 1 << 34, 1 << 20,
        *tiles, own, *factor,
    )
    tiles = forward(own, 1)
    copies, own = local(second_body, 8, [group, tile], 1 << 27, 1 << 20, *tiles, own, *factor)
    tiles = lax.all_to_all(copies, OWNERS, 0, 0)
    copies, own, packed = local(
        third_body, 8, [group, tile, shape(3 * TILES, members, rows)],
        1 << 27, 2 << 20, tiles, own, *factor,
    )
    early = crossings(packed, EARLY)
    received = lax.all_to_all(copies, OWNERS, 0, 0)
    ends = received[(STEPS - 1) * TILES:]
    late = crossings(ends, LATE)
    own, ends, *early = lax.optimization_barrier((own, ends, packed, *early))
    before, partly = local(
        middle_body, 16,
        [shape(members, (STEPS - 1) * WIDTH), shape(blocks, members, rows)],
        1 << 30, 12 << 20, *early, right, panel, inverses,
    )
    last, low, high, sums = local(
        finish_body, 16,
        [shape(members, WIDTH)] + [shape(blocks // 2, members, rows)] * 2 + [shape(2, blocks, rows)],
        1 << 28, 4 << 20, ends, *late, own, partly, panel, inverses,
    )
    sums = sums + lax.ppermute(sums, "core", [(0, 1), (1, 0)])
    others = []
    for change in (1, 2, 3):
        others.append(lax.ppermute(sums, "y", [(i, i ^ change) for i in range(4)]))
    sums = sums + others[0] + (others[1] + others[2])
    solved = jnp.concatenate([before, last], axis=1)
    left = jnp.concatenate([low, high], axis=0)
    size = members * 8
    mean = sums[0] / size
    spread = sums[1] / size - mean * mean
    return (
        solved.T,
        left.transpose(0, 2, 1).reshape(right_side.shape),
        spread.reshape(blocks, 1, rows),
    )


def solution(mesh):
    fine = Mesh(mesh.devices.reshape(SIZES), AXES)
    return jax.shard_map(
        shards,
        mesh=fine,
        in_specs=(P(None, ROWS, None, None), P(None, ROWS, None, MEM), P()),
        out_specs=(P(None, MEM), P(None, ROWS, None, MEM), P(None, ROWS, None)),
        check_vma=False,
    )
```

```python
import jax
import jax.numpy as jnp
from jax import lax
from jax.experimental import pallas as pl
from jax.experimental.pallas import tpu as pltpu
from jax.sharding import Mesh, PartitionSpec as P

f32 = jnp.float32
bf16 = jnp.bfloat16
AXES = ("xh", "xl", "zh", "zl", "y", "core")
SIZES = (2, 2, 2, 4, 4, 2)
ROWS = AXES[:4]
OWNERS = AXES[1:4]
MEM = AXES[4:]
TILES = 4
STEPS = 4
WIDTH = 512
NT = (((1,), (1,)), ((), ()))
NN = (((1,), (0,)), ((), ()))
SOURCES = 2
GROUP = 16
ORDER = (2, 3, 1, 0)


def line_of():
    return lax.axis_index("xh")


def step_of():
    return lax.axis_index("xh") * 4 + lax.axis_index("xl") * 2 + lax.axis_index("zh")


EARLY = [(0, 2), (1, 3)]
LATE = [(0, 3), (1, 2)]


def crossings(value, pairs):
    return [lax.ppermute(value, ROWS[:2], pairs)]


def split(value):
    high = value.astype(bf16)
    return high, (value - high.astype(f32)).astype(bf16)


def dot16(left, right, dims):
    return lax.dot_general(left, right, dims, preferred_element_type=f32)


def joined(ref, first):
    return jnp.concatenate([ref[first + i] for i in range(TILES)], axis=1)


def times_split(value, right):
    return times_halves(value, *split(right))


def times_halves(value, right_high, right_low):
    rows = value.shape[0]
    high, low = split(value)
    wide = dot16(jnp.concatenate([high, low], axis=0), right_high, NT)
    return wide[:rows] + wide[rows:] + dot16(high, right_low, NT)


def chosen(line, refs, first):
    value = joined(refs[0], first)
    for at, ref in enumerate(refs[1:]):
        value = jnp.where(line == at + 1, joined(ref, first), value)
    return value


def product_halves(part, inverse):
    high, low = split(part)
    inverse_high, inverse_low = split(inverse)
    wide = dot16(jnp.concatenate([high, low], axis=0), inverse_high, NN)
    rows = high.shape[0]
    return split(wide[:rows] + wide[rows:] + dot16(high, inverse_low, NN))


def prepare_body(part_ref, inverse_ref, high_ref, low_ref):
    high_ref[...], low_ref[...] = product_halves(part_ref[...], inverse_ref[...])


def complete_body(panel_ref, inverses_ref, high_ref, low_ref):
    for step in range(1, STEPS - 1):
        part = panel_ref[0, :, step * WIDTH:(step + 1) * WIDTH]
        columns = slice((step - 1) * WIDTH, step * WIDTH)
        high_ref[:, columns], low_ref[:, columns] = product_halves(part, inverses_ref[step])


def arrived(lane, refs, at):
    tiles = []
    for tile in range(TILES):
        wanted = jnp.bitwise_xor(lane, tile)
        value = refs[0][at]
        for change, ref in zip(ORDER[1:], refs[1:]):
            value = jnp.where(wanted == change, ref[at], value)
        tiles.append(value)
    return tiles


def advanced(own_ref, high_refs, low_refs, tiles):
    steps = len(tiles) // TILES
    high, low = (
        jnp.concatenate([ref[...] for ref in refs], axis=1)[:, :steps * WIDTH]
        for refs in (high_refs, low_refs)
    )
    change = times_halves(jnp.concatenate(tiles, axis=1), high, low)
    return jnp.where(step_of() == steps, own_ref[...] - change, own_ref[...])


def first_body(r0, r1, r2, r3, own_ref, high_ref, low_ref, own_out_ref):
    tiles = arrived(lax.axis_index("zl"), (r0, r1, r2, r3), 0)
    own_out_ref[0] = advanced(own_ref, [high_ref], [low_ref], tiles)


def second_body(r0, r1, r2, r3, f0, f1, f2, f3, own_ref, h0, l0, h1, l1, copies_ref, own_out_ref):
    lane = lax.axis_index("zl")
    tiles = arrived(lane, (f0, f1, f2, f3), 0) + arrived(lane, (r0, r1, r2, r3), 0)
    own = advanced(own_ref.at[0], [h0, h1], [l0, l1], tiles)
    own_out_ref[...] = own
    for i in range(GROUP):
        copies_ref[i] = own


def third_body(tiles_ref, own_ref, h0, l0, h1, l1, copies_ref, own_out_ref, packed_ref):
    tiles = [tiles_ref[i] for i in range((STEPS - 1) * TILES)]
    own = advanced(own_ref, [h0, h1], [l0, l1], tiles)
    own_out_ref[...] = own
    for i in range(GROUP):
        copies_ref[i] = own
    for i, value in enumerate(tiles):
        packed_ref[i] = value


def middle_body(*refs):
    sources = refs[:SOURCES]
    right_ref, panel_ref, inverses_ref = refs[SOURCES:SOURCES + 3]
    solved_ref, left_ref = refs[-2:]
    parts = []
    for step in range(STEPS - 1):
        solved = times_split(chosen(line_of(), sources, step * TILES), inverses_ref[step])
        solved_ref[:, step * WIDTH:(step + 1) * WIDTH] = solved
        parts.append(solved)
    solved = jnp.concatenate(parts, axis=1)
    for block in range(right_ref.shape[0]):
        product = times_split(solved, panel_ref[block, :, :(STEPS - 1) * WIDTH])
        left_ref[block] = right_ref[block] - product


def finish_body(*refs):
    sources = refs[:SOURCES]
    own_ref, partly_ref, panel_ref, inverses_ref = refs[SOURCES:SOURCES + 4]
    solved_ref, low_ref, high_ref, sums_ref = refs[-4:]
    step = STEPS - 1
    solved = times_split(chosen(line_of(), sources, 0), inverses_ref[step])
    solved_ref[...] = solved
    for block in range(partly_ref.shape[0]):
        product = times_split(solved, panel_ref[block, :, step * WIDTH:])
        left = partly_ref[block] - product
        if block == 0:
            left = jnp.where(step_of() < STEPS, own_ref[...], left)
        half = low_ref if 2 * block < partly_ref.shape[0] else high_ref
        half[block % half.shape[0]] = left
        sums_ref[0, block:block + 1] = jnp.sum(left, axis=0, keepdims=True)
        sums_ref[1, block:block + 1] = jnp.sum(left * left, axis=0, keepdims=True)


VMEM = pl.BlockSpec(memory_space=pltpu.VMEM)


def shape(*dims):
    return jax.ShapeDtypeStruct(dims, f32)


def params(limit):
    return pltpu.CompilerParams(vmem_limit_bytes=limit << 20)


def cost(flops, size):
    return pl.CostEstimate(flops=flops, bytes_accessed=size, transcendentals=0)


def local(body, limit, outs, flops, size, *args):
    return pl.pallas_call(
        body,
        out_shape=outs,
        in_specs=[VMEM] * len(args),
        out_specs=[VMEM] * len(outs),
        compiler_params=params(limit),
        cost_estimate=cost(flops, size),
    )(*args)


def forward(value, source, target):
    pieces = []
    for change in ORDER:
        pieces.append(lax.ppermute(
            value, ROWS, [(source + i, target + (i ^ change)) for i in range(TILES)]
        ))
    return pieces


def shards(factor_panel, right_side, inverses):
    blocks, _, rows, columns = factor_panel.shape
    members = right_side.shape[3]
    panel = factor_panel.reshape(blocks, rows, columns)
    right = right_side.reshape(blocks, rows, members).transpose(0, 2, 1)
    tile = shape(members, rows)
    group = shape(GROUP, members, rows)

    own = right[0]
    own = own[None]
    tiles = forward(own, 0, TILES)
    far = forward(own, 0, 2 * TILES)
    half = jax.ShapeDtypeStruct((rows, WIDTH), bf16)
    factor = local(
        prepare_body, 16, [half, half], 1 << 28, 2 << 20,
        panel[0, :, :WIDTH], inverses[0],
    )
    own, = local(
        first_body, 8, [shape(1, members, rows)], 1 << 33, 1 << 20,
        *tiles, own[0], *factor,
    )
    tiles = forward(own, TILES, 2 * TILES)
    half = jax.ShapeDtypeStruct((rows, (STEPS - 2) * WIDTH), bf16)
    factor += local(complete_body, 16, [half, half], 1 << 29, 12 << 20, panel, inverses)
    copies, own = local(second_body, 8, [group, tile], 1 << 27, 1 << 20, *tiles, *far, own, *factor)
    tiles = lax.all_to_all(copies, OWNERS, 0, 0)
    copies, own, packed = local(
        third_body, 8, [group, tile, shape(3 * TILES, members, rows)],
        1 << 27, 2 << 20, tiles, own, *factor,
    )
    early = crossings(packed, EARLY)
    received = lax.all_to_all(copies, OWNERS, 0, 0)
    ends = received[(STEPS - 1) * TILES:]
    late = crossings(ends, LATE)
    own, ends, *early = lax.optimization_barrier((own, ends, packed, *early))
    before, partly = local(
        middle_body, 16,
        [shape(members, (STEPS - 1) * WIDTH), shape(blocks, members, rows)],
        1 << 30, 12 << 20, *early, right, panel, inverses,
    )
    last, low, high, sums = local(
        finish_body, 16,
        [shape(members, WIDTH)] + [shape(blocks // 2, members, rows)] * 2 + [shape(2, blocks, rows)],
        1 << 28, 4 << 20, ends, *late, own, partly, panel, inverses,
    )
    sums = sums + lax.ppermute(sums, "core", [(0, 1), (1, 0)])
    others = []
    for change in (1, 2, 3):
        others.append(lax.ppermute(sums, "y", [(i, i ^ change) for i in range(4)]))
    sums = sums + others[0] + (others[1] + others[2])
    solved = jnp.concatenate([before, last], axis=1)
    left = jnp.concatenate([low, high], axis=0)
    size = members * 8
    mean = sums[0] / size
    spread = sums[1] / size - mean * mean
    return (
        solved.T,
        left.transpose(0, 2, 1).reshape(right_side.shape),
        spread.reshape(blocks, 1, rows),
    )


def solution(mesh):
    fine = Mesh(mesh.devices.reshape(SIZES), AXES)
    return jax.shard_map(
        shards,
        mesh=fine,
        in_specs=(P(None, ROWS, None, None), P(None, ROWS, None, MEM), P()),
        out_specs=(P(None, MEM), P(None, ROWS, None, MEM), P(None, ROWS, None)),
        check_vma=False,
    )
```

```python
import jax
import jax.numpy as jnp
from jax import lax
from jax.experimental import pallas as pl
from jax.experimental.pallas import tpu as pltpu
from jax.sharding import Mesh, PartitionSpec as P

f32 = jnp.float32
bf16 = jnp.bfloat16
AXES = ("xh", "xl", "zh", "zl", "y", "core")
SIZES = (2, 2, 2, 4, 4, 2)
ROWS = AXES[:4]
OWNERS = AXES[1:4]
MEM = AXES[4:]
TILES = 4
STEPS = 4
WIDTH = 512
NT = (((1,), (1,)), ((), ()))
NN = (((1,), (0,)), ((), ()))
SOURCES = 2
GROUP = 16
ORDER = (2, 3, 1, 0)


def line_of():
    return lax.axis_index("xh")


def step_of():
    return lax.axis_index("xh") * 4 + lax.axis_index("xl") * 2 + lax.axis_index("zh")


EARLY = [(0, 2), (1, 3)]
LATE = [(0, 3), (1, 2)]


def crossings(value, pairs):
    return [lax.ppermute(value, ROWS[:2], pairs)]


def split(value):
    high = value.astype(bf16)
    return high, (value - high.astype(f32)).astype(bf16)


def dot16(left, right, dims):
    return lax.dot_general(left, right, dims, preferred_element_type=f32)


def joined(ref, first):
    return jnp.concatenate([ref[first + i] for i in range(TILES)], axis=1)


def times_split(value, right):
    return times_halves(value, *split(right))


def times_halves(value, right_high, right_low):
    rows = value.shape[0]
    high, low = split(value)
    wide = dot16(jnp.concatenate([high, low], axis=0), right_high, NT)
    return wide[:rows] + wide[rows:] + dot16(high, right_low, NT)


def chosen(line, refs, first):
    value = joined(refs[0], first)
    for at, ref in enumerate(refs[1:]):
        value = jnp.where(line == at + 1, joined(ref, first), value)
    return value


def product_halves(part, inverse):
    high, low = split(part)
    inverse_high, inverse_low = split(inverse)
    wide = dot16(jnp.concatenate([high, low], axis=0), inverse_high, NN)
    rows = high.shape[0]
    return split(wide[:rows] + wide[rows:] + dot16(high, inverse_low, NN))


def prepare_body(part_ref, inverse_ref, high_ref, low_ref):
    high_ref[...], low_ref[...] = product_halves(part_ref[...], inverse_ref[...])


def complete_body(panel_ref, inverses_ref, high_ref, low_ref):
    for step in range(1, STEPS - 1):
        part = panel_ref[0, :, step * WIDTH:(step + 1) * WIDTH]
        columns = slice((step - 1) * WIDTH, step * WIDTH)
        high_ref[:, columns], low_ref[:, columns] = product_halves(part, inverses_ref[step])


def arrived(lane, refs, at):
    tiles = []
    for tile in range(TILES):
        wanted = jnp.bitwise_xor(lane, tile)
        value = refs[0][at]
        for change, ref in zip(ORDER[1:], refs[1:]):
            value = jnp.where(wanted == change, ref[at], value)
        tiles.append(value)
    return tiles


def advanced(own_ref, high_refs, low_refs, tiles):
    steps = len(tiles) // TILES
    high, low = (
        jnp.concatenate([ref[...] for ref in refs], axis=1)[:, :steps * WIDTH]
        for refs in (high_refs, low_refs)
    )
    change = times_halves(jnp.concatenate(tiles, axis=1), high, low)
    return jnp.where(step_of() == steps, own_ref[...] - change, own_ref[...])


def first_body(r0, r1, r2, r3, own_ref, high_ref, low_ref, own_out_ref):
    tiles = arrived(lax.axis_index("zl"), (r0, r1, r2, r3), 0)
    own_out_ref[0] = advanced(own_ref, [high_ref], [low_ref], tiles)


def second_body(r0, r1, r2, r3, f0, f1, f2, f3, own_ref, h0, l0, h1, l1, copies_ref, own_out_ref):
    lane = lax.axis_index("zl")
    tiles = arrived(lane, (f0, f1, f2, f3), 0) + arrived(lane, (r0, r1, r2, r3), 0)
    own = advanced(own_ref.at[0], [h0, h1], [l0, l1], tiles)
    own_out_ref[...] = own
    for i in range(GROUP):
        copies_ref[i] = own


def third_body(tiles_ref, own_ref, h0, l0, h1, l1, copies_ref, own_out_ref, packed_ref):
    tiles = [tiles_ref[i] for i in range((STEPS - 1) * TILES)]
    own = advanced(own_ref, [h0, h1], [l0, l1], tiles)
    own_out_ref[...] = own
    for i in range(GROUP):
        copies_ref[i] = own
    for i, value in enumerate(tiles):
        packed_ref[i] = value


def middle_body(*refs):
    sources = refs[:SOURCES]
    right_ref, panel_ref, inverses_ref = refs[SOURCES:SOURCES + 3]
    solved_ref, left_ref = refs[-2:]
    parts = []
    for step in range(STEPS - 1):
        solved = times_split(chosen(line_of(), sources, step * TILES), inverses_ref[step])
        solved_ref[:, step * WIDTH:(step + 1) * WIDTH] = solved
        parts.append(solved)
    solved = jnp.concatenate(parts, axis=1)
    for block in range(right_ref.shape[0]):
        product = times_split(solved, panel_ref[block, :, :(STEPS - 1) * WIDTH])
        left_ref[block] = right_ref[block] - product


def finish_body(*refs):
    sources = refs[:SOURCES]
    own_ref, partly_ref, panel_ref, inverses_ref = refs[SOURCES:SOURCES + 4]
    solved_ref, low_ref, high_ref, sums_ref = refs[-4:]
    step = STEPS - 1
    solved = times_split(chosen(line_of(), sources, 0), inverses_ref[step])
    solved_ref[...] = solved
    for block in range(partly_ref.shape[0]):
        product = times_split(solved, panel_ref[block, :, step * WIDTH:])
        left = partly_ref[block] - product
        if block == 0:
            left = jnp.where(step_of() < STEPS, own_ref[...], left)
        half = low_ref if 2 * block < partly_ref.shape[0] else high_ref
        half[block % half.shape[0]] = left
        sums_ref[0, block:block + 1] = jnp.sum(left, axis=0, keepdims=True)
        sums_ref[1, block:block + 1] = jnp.sum(left * left, axis=0, keepdims=True)


VMEM = pl.BlockSpec(memory_space=pltpu.VMEM)


def shape(*dims):
    return jax.ShapeDtypeStruct(dims, f32)


def params(limit):
    return pltpu.CompilerParams(vmem_limit_bytes=limit << 20)


def cost(flops, size):
    return pl.CostEstimate(flops=flops, bytes_accessed=size, transcendentals=0)


def local(body, limit, outs, flops, size, *args):
    return pl.pallas_call(
        body,
        out_shape=outs,
        in_specs=[VMEM] * len(args),
        out_specs=[VMEM] * len(outs),
        compiler_params=params(limit),
        cost_estimate=cost(flops, size),
    )(*args)


def forward(value, source, target):
    pieces = []
    for change in ORDER:
        pieces.append(lax.ppermute(
            value, ROWS, [(source + i, target + (i ^ change)) for i in range(TILES)]
        ))
    return pieces


def shards(factor_panel, right_side, inverses):
    blocks, _, rows, columns = factor_panel.shape
    members = right_side.shape[3]
    panel = factor_panel.reshape(blocks, rows, columns)
    right = right_side.reshape(blocks, rows, members).transpose(0, 2, 1)
    tile = shape(members, rows)
    group = shape(GROUP, members, rows)

    own = right[0]
    own = own[None]
    tiles = forward(own, 0, TILES)
    far = forward(own, 0, 2 * TILES)
    half = jax.ShapeDtypeStruct((rows, WIDTH), bf16)
    factor = local(
        prepare_body, 16, [half, half], 1 << 28, 2 << 20,
        panel[0, :, :WIDTH], inverses[0],
    )
    own, = local(
        first_body, 8, [shape(1, members, rows)], 1 << 33, 1 << 20,
        *tiles, own[0], *factor,
    )
    tiles = forward(own, TILES, 2 * TILES)
    half = jax.ShapeDtypeStruct((rows, (STEPS - 2) * WIDTH), bf16)
    factor += local(complete_body, 16, [half, half], 1 << 29, 12 << 20, panel, inverses)
    copies, own = local(second_body, 8, [group, tile], 1 << 27, 1 << 20, *tiles, *far, own, *factor)
    tiles = lax.all_to_all(copies, OWNERS, 0, 0)
    copies, own, packed = local(
        third_body, 8, [group, tile, shape(3 * TILES, members, rows)],
        1 << 27, 2 << 20, tiles, own, *factor,
    )
    early = crossings(packed, EARLY)
    received = lax.all_to_all(copies, OWNERS, 0, 0)
    ends = received[(STEPS - 1) * TILES:]
    late = crossings(ends, LATE)
    own, ends, *early = lax.optimization_barrier((own, ends, packed, *early))
    before, partly = local(
        middle_body, 16,
        [shape(members, (STEPS - 1) * WIDTH), shape(blocks, members, rows)],
        1 << 30, 12 << 20, *early, right, panel, inverses,
    )
    last, low, high, sums = local(
        finish_body, 16,
        [shape(members, WIDTH)] + [shape(blocks // 2, members, rows)] * 2 + [shape(2, blocks, rows)],
        1 << 28, 4 << 20, ends, *late, own, partly, panel, inverses,
    )
    sums = sums + lax.ppermute(sums, "core", [(0, 1), (1, 0)])
    for change in (1, 3):
        sums = sums + lax.ppermute(sums, "y", [(i, i ^ change) for i in range(4)])
    solved = jnp.concatenate([before, last], axis=1)
    left = jnp.concatenate([low, high], axis=0)
    size = members * 8
    mean = sums[0] / size
    spread = sums[1] / size - mean * mean
    return (
        solved.T,
        left.transpose(0, 2, 1).reshape(right_side.shape),
        spread.reshape(blocks, 1, rows),
    )


def solution(mesh):
    fine = Mesh(mesh.devices.reshape(SIZES), AXES)
    return jax.shard_map(
        shards,
        mesh=fine,
        in_specs=(P(None, ROWS, None, None), P(None, ROWS, None, MEM), P()),
        out_specs=(P(None, MEM), P(None, ROWS, None, MEM), P(None, ROWS, None)),
        check_vma=False,
    )
```

```python
import jax
import jax.numpy as jnp
from jax import lax
from jax.experimental import pallas as pl
from jax.experimental.pallas import tpu as pltpu
from jax.sharding import Mesh, PartitionSpec as P

f32 = jnp.float32
bf16 = jnp.bfloat16
AXES = ("xh", "xl", "zh", "zl", "y", "core")
SIZES = (2, 2, 2, 4, 4, 2)
ROWS = AXES[:4]
OWNERS = AXES[1:4]
MEM = AXES[4:]
TILES = 4
STEPS = 4
WIDTH = 512
NT = (((1,), (1,)), ((), ()))
NN = (((1,), (0,)), ((), ()))
SOURCES = 2
GROUP = 16
ORDER = (2, 3, 1, 0)
PAIRS = (2, 0)


def line_of():
    return lax.axis_index("xh")


def step_of():
    return lax.axis_index("xh") * 4 + lax.axis_index("xl") * 2 + lax.axis_index("zh")


EARLY = [(0, 2), (1, 3)]
LATE = [(0, 3), (1, 2)]


def crossings(value, pairs):
    return [lax.ppermute(value, ROWS[:2], pairs)]


def split(value):
    high = value.astype(bf16)
    return high, (value - high.astype(f32)).astype(bf16)


def dot16(left, right, dims):
    return lax.dot_general(left, right, dims, preferred_element_type=f32)


def joined(ref, first):
    return jnp.concatenate([ref[first + i] for i in range(TILES)], axis=1)


def times_split(value, right):
    return times_halves(value, *split(right))


def times_halves(value, right_high, right_low):
    rows = value.shape[0]
    high, low = split(value)
    wide = dot16(jnp.concatenate([high, low], axis=0), right_high, NT)
    return wide[:rows] + wide[rows:] + dot16(high, right_low, NT)


def chosen(line, refs, first):
    value = joined(refs[0], first)
    for at, ref in enumerate(refs[1:]):
        value = jnp.where(line == at + 1, joined(ref, first), value)
    return value


def product_halves(part, inverse):
    high, low = split(part)
    inverse_high, inverse_low = split(inverse)
    wide = dot16(jnp.concatenate([high, low], axis=0), inverse_high, NN)
    rows = high.shape[0]
    return split(wide[:rows] + wide[rows:] + dot16(high, inverse_low, NN))


def prepare_body(part_ref, inverse_ref, high_ref, low_ref):
    high_ref[...], low_ref[...] = product_halves(part_ref[...], inverse_ref[...])


def complete_body(panel_ref, inverses_ref, high_ref, low_ref):
    for step in range(1, STEPS - 1):
        part = panel_ref[0, :, step * WIDTH:(step + 1) * WIDTH]
        columns = slice((step - 1) * WIDTH, step * WIDTH)
        high_ref[:, columns], low_ref[:, columns] = product_halves(part, inverses_ref[step])


def arrived(lane, refs, at):
    tiles = []
    for tile in range(TILES):
        wanted = jnp.bitwise_xor(lane, tile)
        value = refs[0][at]
        for change, ref in zip(ORDER[1:], refs[1:]):
            value = jnp.where(wanted == change, ref[at], value)
        tiles.append(value)
    return tiles


def advanced(own_ref, high_refs, low_refs, tiles):
    steps = len(tiles) // TILES
    high, low = (
        jnp.concatenate([ref[...] for ref in refs], axis=1)[:, :steps * WIDTH]
        for refs in (high_refs, low_refs)
    )
    change = times_halves(jnp.concatenate(tiles, axis=1), high, low)
    return jnp.where(step_of() == steps, own_ref[...] - change, own_ref[...])


def paired(lane, near_ref, across_ref):
    tiles = []
    for tile in range(TILES):
        wanted = jnp.bitwise_xor(lane, tile)
        value = near_ref[0]
        for change, other in ((1, near_ref[1]), (2, across_ref[0]), (3, across_ref[1])):
            value = jnp.where(wanted == change, other, value)
        tiles.append(value)
    return tiles


def first_body(across_ref, near_ref, own_ref, high_ref, low_ref, own_out_ref):
    tiles = paired(lax.axis_index("zl"), near_ref, across_ref)
    own_out_ref[0] = advanced(own_ref, [high_ref], [low_ref], tiles)


def second_body(r0, r1, r2, r3, across_ref, near_ref, own_ref, h0, l0, h1, l1, copies_ref,
                own_out_ref):
    lane = lax.axis_index("zl")
    tiles = paired(lane, near_ref, across_ref) + arrived(lane, (r0, r1, r2, r3), 0)
    own = advanced(own_ref.at[0], [h0, h1], [l0, l1], tiles)
    own_out_ref[...] = own
    for i in range(GROUP):
        copies_ref[i] = own


def third_body(tiles_ref, own_ref, h0, l0, h1, l1, copies_ref, own_out_ref, packed_ref):
    tiles = [tiles_ref[i] for i in range((STEPS - 1) * TILES)]
    own = advanced(own_ref, [h0, h1], [l0, l1], tiles)
    own_out_ref[...] = own
    for i in range(GROUP):
        copies_ref[i] = own
    for i, value in enumerate(tiles):
        packed_ref[i] = value


def middle_body(*refs):
    sources = refs[:SOURCES]
    right_ref, panel_ref, inverses_ref = refs[SOURCES:SOURCES + 3]
    solved_ref, left_ref = refs[-2:]
    parts = []
    for step in range(STEPS - 1):
        solved = times_split(chosen(line_of(), sources, step * TILES), inverses_ref[step])
        solved_ref[:, step * WIDTH:(step + 1) * WIDTH] = solved
        parts.append(solved)
    solved = jnp.concatenate(parts, axis=1)
    for block in range(right_ref.shape[0]):
        product = times_split(solved, panel_ref[block, :, :(STEPS - 1) * WIDTH])
        left_ref[block] = right_ref[block] - product


def finish_body(*refs):
    sources = refs[:SOURCES]
    own_ref, partly_ref, panel_ref, inverses_ref = refs[SOURCES:SOURCES + 4]
    solved_ref, low_ref, high_ref, sums_ref = refs[-4:]
    step = STEPS - 1
    solved = times_split(chosen(line_of(), sources, 0), inverses_ref[step])
    solved_ref[...] = solved
    for block in range(partly_ref.shape[0]):
        product = times_split(solved, panel_ref[block, :, step * WIDTH:])
        left = partly_ref[block] - product
        if block == 0:
            left = jnp.where(step_of() < STEPS, own_ref[...], left)
        half = low_ref if 2 * block < partly_ref.shape[0] else high_ref
        half[block % half.shape[0]] = left
        sums_ref[0, block:block + 1] = jnp.sum(left, axis=0, keepdims=True)
        sums_ref[1, block:block + 1] = jnp.sum(left * left, axis=0, keepdims=True)


VMEM = pl.BlockSpec(memory_space=pltpu.VMEM)


def shape(*dims):
    return jax.ShapeDtypeStruct(dims, f32)


def params(limit):
    return pltpu.CompilerParams(vmem_limit_bytes=limit << 20)


def cost(flops, size):
    return pl.CostEstimate(flops=flops, bytes_accessed=size, transcendentals=0)


def local(body, limit, outs, flops, size, *args):
    return pl.pallas_call(
        body,
        out_shape=outs,
        in_specs=[VMEM] * len(args),
        out_specs=[VMEM] * len(outs),
        compiler_params=params(limit),
        cost_estimate=cost(flops, size),
    )(*args)


def forward(value, source, target, order):
    pieces = []
    for change in order:
        pieces.append(lax.ppermute(
            value, ROWS, [(source + i, target + (i ^ change)) for i in range(TILES)]
        ))
    return pieces


def shards(factor_panel, right_side, inverses):
    blocks, _, rows, columns = factor_panel.shape
    members = right_side.shape[3]
    panel = factor_panel.reshape(blocks, rows, columns)
    right = right_side.reshape(blocks, rows, members).transpose(0, 2, 1)
    tile = shape(members, rows)
    group = shape(GROUP, members, rows)

    own = right[0]
    partner = lax.ppermute(own, ROWS, [(i, i ^ 1) for i in range(TILES)])
    pair = jnp.stack([own, partner])
    tiles = forward(pair, 0, TILES, PAIRS)
    far = forward(pair, 0, 2 * TILES, PAIRS)
    half = jax.ShapeDtypeStruct((rows, WIDTH), bf16)
    part, inverse = panel[0, :, :WIDTH], inverses[0]
    factor = local(
        prepare_body, 16, [half, half], 1 << 28, 2 << 20,
        part, inverse,
    )
    own, = local(
        first_body, 8, [shape(1, members, rows)], 1 << 33, 1 << 20,
        *tiles, own, *factor,
    )
    tiles = forward(own, TILES, 2 * TILES, ORDER)
    half = jax.ShapeDtypeStruct((rows, (STEPS - 2) * WIDTH), bf16)
    factor += local(complete_body, 16, [half, half], 1 << 29, 12 << 20, panel, inverses)
    copies, own = local(second_body, 8, [group, tile], 1 << 27, 1 << 20, *tiles, *far, own, *factor)
    tiles = lax.all_to_all(copies, OWNERS, 0, 0)
    copies, own, packed = local(
        third_body, 8, [group, tile, shape(3 * TILES, members, rows)],
        1 << 27, 2 << 20, tiles, own, *factor,
    )
    early = crossings(packed, EARLY)
    received = lax.all_to_all(copies, OWNERS, 0, 0)
    ends = received[(STEPS - 1) * TILES:]
    late = crossings(ends, LATE)
    own, ends, *early = lax.optimization_barrier((own, ends, packed, *early))
    before, partly = local(
        middle_body, 16,
        [shape(members, (STEPS - 1) * WIDTH), shape(blocks, members, rows)],
        1 << 30, 12 << 20, *early, right, panel, inverses,
    )
    last, low, high, sums = local(
        finish_body, 16,
        [shape(members, WIDTH)] + [shape(blocks // 2, members, rows)] * 2 + [shape(2, blocks, rows)],
        1 << 28, 4 << 20, ends, *late, own, partly, panel, inverses,
    )
    sums = sums + lax.ppermute(sums, "core", [(0, 1), (1, 0)])
    for change in (1, 3):
        sums = sums + lax.ppermute(sums, "y", [(i, i ^ change) for i in range(4)])
    solved = jnp.concatenate([before, last], axis=1)
    left = jnp.concatenate([low, high], axis=0)
    size = members * 8
    mean = sums[0] / size
    spread = sums[1] / size - mean * mean
    return (
        solved.T,
        left.transpose(0, 2, 1).reshape(right_side.shape),
        spread.reshape(blocks, 1, rows),
    )


def solution(mesh):
    fine = Mesh(mesh.devices.reshape(SIZES), AXES)
    return jax.shard_map(
        shards,
        mesh=fine,
        in_specs=(P(None, ROWS, None, None), P(None, ROWS, None, MEM), P()),
        out_specs=(P(None, MEM), P(None, ROWS, None, MEM), P(None, ROWS, None)),
        check_vma=False,
    )
```

```python
import jax
import jax.numpy as jnp
from jax import lax
from jax.experimental import pallas as pl
from jax.experimental.pallas import tpu as pltpu
from jax.sharding import Mesh, PartitionSpec as P

f32 = jnp.float32
bf16 = jnp.bfloat16
AXES = ("xh", "xl", "zh", "zl", "y", "core")
SIZES = (2, 2, 2, 4, 4, 2)
ROWS = AXES[:4]
OWNERS = AXES[1:4]
MEM = AXES[4:]
TILES = 4
STEPS = 4
WIDTH = 512
NT = (((1,), (1,)), ((), ()))
NN = (((1,), (0,)), ((), ()))
SOURCES = 2
GROUP = 16
ORDER = (2, 3, 1, 0)
PAIRS = (2, 0)


def line_of():
    return lax.axis_index("xh")


def step_of():
    return lax.axis_index("xh") * 4 + lax.axis_index("xl") * 2 + lax.axis_index("zh")


EARLY = [(0, 2), (1, 3)]
LATE = [(0, 3), (1, 2)]


def crossings(value, pairs):
    return [lax.ppermute(value, ROWS[:2], pairs)]


def split(value):
    high = value.astype(bf16)
    return high, (value - high.astype(f32)).astype(bf16)


def dot16(left, right, dims):
    return lax.dot_general(left, right, dims, preferred_element_type=f32)


def joined(ref, first):
    return jnp.concatenate([ref[first + i] for i in range(TILES)], axis=1)


def times_split(value, right):
    return times_halves(value, *split(right))


def times_halves(value, right_high, right_low):
    rows = value.shape[0]
    high, low = split(value)
    wide = dot16(jnp.concatenate([high, low], axis=0), right_high, NT)
    return wide[:rows] + wide[rows:] + dot16(high, right_low, NT)


def chosen(line, refs, first):
    value = joined(refs[0], first)
    for at, ref in enumerate(refs[1:]):
        value = jnp.where(line == at + 1, joined(ref, first), value)
    return value


def product_halves(part, inverse):
    high, low = split(part)
    inverse_high, inverse_low = split(inverse)
    wide = dot16(jnp.concatenate([high, low], axis=0), inverse_high, NN)
    rows = high.shape[0]
    return split(wide[:rows] + wide[rows:] + dot16(high, inverse_low, NN))


def prepare_body(part_ref, inverse_ref, high_ref, low_ref):
    high_ref[...], low_ref[...] = product_halves(part_ref[...], inverse_ref[...])


def complete_body(panel_ref, inverses_ref, high_ref, low_ref, tail_high_ref, tail_low_ref):
    for step in range(1, STEPS - 1):
        part = panel_ref[0, :, step * WIDTH:(step + 1) * WIDTH]
        columns = slice((step - 1) * WIDTH, step * WIDTH)
        high_ref[:, columns], low_ref[:, columns] = product_halves(part, inverses_ref[step])
    last = STEPS - 1
    for block in range(panel_ref.shape[0]):
        part = panel_ref[block, :, last * WIDTH:]
        tail_high_ref[block], tail_low_ref[block] = product_halves(part, inverses_ref[last])


def arrived(lane, refs, at):
    tiles = []
    for tile in range(TILES):
        wanted = jnp.bitwise_xor(lane, tile)
        value = refs[0][at]
        for change, ref in zip(ORDER[1:], refs[1:]):
            value = jnp.where(wanted == change, ref[at], value)
        tiles.append(value)
    return tiles


def advanced(own_ref, high_refs, low_refs, tiles):
    steps = len(tiles) // TILES
    high, low = (
        jnp.concatenate([ref[...] for ref in refs], axis=1)[:, :steps * WIDTH]
        for refs in (high_refs, low_refs)
    )
    change = times_halves(jnp.concatenate(tiles, axis=1), high, low)
    return jnp.where(step_of() == steps, own_ref[...] - change, own_ref[...])


def paired(lane, near_ref, across_ref):
    tiles = []
    for tile in range(TILES):
        wanted = jnp.bitwise_xor(lane, tile)
        value = near_ref[0]
        for change, other in ((1, near_ref[1]), (2, across_ref[0]), (3, across_ref[1])):
            value = jnp.where(wanted == change, other, value)
        tiles.append(value)
    return tiles


def first_body(across_ref, near_ref, own_ref, high_ref, low_ref, own_out_ref):
    tiles = paired(lax.axis_index("zl"), near_ref, across_ref)
    own_out_ref[0] = advanced(own_ref, [high_ref], [low_ref], tiles)


def second_body(r0, r1, r2, r3, across_ref, near_ref, own_ref, h0, l0, h1, l1, copies_ref,
                own_out_ref):
    lane = lax.axis_index("zl")
    tiles = paired(lane, near_ref, across_ref) + arrived(lane, (r0, r1, r2, r3), 0)
    own = advanced(own_ref.at[0], [h0, h1], [l0, l1], tiles)
    own_out_ref[...] = own
    for i in range(GROUP):
        copies_ref[i] = own


def third_body(tiles_ref, own_ref, h0, l0, h1, l1, copies_ref, own_out_ref, packed_ref):
    tiles = [tiles_ref[i] for i in range((STEPS - 1) * TILES)]
    own = advanced(own_ref, [h0, h1], [l0, l1], tiles)
    own_out_ref[...] = own
    for i in range(GROUP):
        copies_ref[i] = own
    for i, value in enumerate(tiles):
        packed_ref[i] = value


def middle_body(*refs):
    sources = refs[:SOURCES]
    right_ref, panel_ref, inverses_ref = refs[SOURCES:SOURCES + 3]
    solved_ref, left_ref = refs[-2:]
    parts = []
    for step in range(STEPS - 1):
        solved = times_split(chosen(line_of(), sources, step * TILES), inverses_ref[step])
        solved_ref[:, step * WIDTH:(step + 1) * WIDTH] = solved
        parts.append(solved)
    solved = jnp.concatenate(parts, axis=1)
    for block in range(right_ref.shape[0]):
        product = times_split(solved, panel_ref[block, :, :(STEPS - 1) * WIDTH])
        left_ref[block] = right_ref[block] - product


def last_body(*refs):
    *sources, inverses_ref, solved_ref = refs
    solved_ref[...] = times_split(chosen(line_of(), sources, 0), inverses_ref[STEPS - 1])


def finish_body(*refs):
    sources = refs[:SOURCES]
    own_ref, partly_ref, tail_high_ref, tail_low_ref = refs[SOURCES:SOURCES + 4]
    low_ref, high_ref, sums_ref = refs[-3:]
    residual = chosen(line_of(), sources, 0)
    for block in range(partly_ref.shape[0]):
        product = times_halves(residual, tail_high_ref[block], tail_low_ref[block])
        left = partly_ref[block] - product
        if block == 0:
            left = jnp.where(step_of() < STEPS, own_ref[...], left)
        half = low_ref if 2 * block < partly_ref.shape[0] else high_ref
        half[block % half.shape[0]] = left
        sums_ref[0, block:block + 1] = jnp.sum(left, axis=0, keepdims=True)
        sums_ref[1, block:block + 1] = jnp.sum(left * left, axis=0, keepdims=True)


VMEM = pl.BlockSpec(memory_space=pltpu.VMEM)


def shape(*dims):
    return jax.ShapeDtypeStruct(dims, f32)


def params(limit):
    return pltpu.CompilerParams(vmem_limit_bytes=limit << 20)


def cost(flops, size):
    return pl.CostEstimate(flops=flops, bytes_accessed=size, transcendentals=0)


def local(body, limit, outs, flops, size, *args):
    return pl.pallas_call(
        body,
        out_shape=outs,
        in_specs=[VMEM] * len(args),
        out_specs=[VMEM] * len(outs),
        compiler_params=params(limit),
        cost_estimate=cost(flops, size),
    )(*args)


def forward(value, source, target, order):
    pieces = []
    for change in order:
        pieces.append(lax.ppermute(
            value, ROWS, [(source + i, target + (i ^ change)) for i in range(TILES)]
        ))
    return pieces


def shards(factor_panel, right_side, inverses):
    blocks, _, rows, columns = factor_panel.shape
    members = right_side.shape[3]
    panel = factor_panel.reshape(blocks, rows, columns)
    right = right_side.reshape(blocks, rows, members).transpose(0, 2, 1)
    tile = shape(members, rows)
    group = shape(GROUP, members, rows)

    own = right[0]
    partner = lax.ppermute(own, ROWS, [(i, i ^ 1) for i in range(TILES)])
    pair = jnp.stack([own, partner])
    tiles = forward(pair, 0, TILES, PAIRS)
    far = forward(pair, 0, 2 * TILES, PAIRS)
    half = jax.ShapeDtypeStruct((rows, WIDTH), bf16)
    part, inverse = panel[0, :, :WIDTH], inverses[0]
    factor = local(
        prepare_body, 16, [half, half], 1 << 28, 2 << 20,
        part, inverse,
    )
    own, = local(
        first_body, 8, [shape(1, members, rows)], 1 << 33, 1 << 20,
        *tiles, own, *factor,
    )
    tiles = forward(own, TILES, 2 * TILES, ORDER)
    half = jax.ShapeDtypeStruct((rows, (STEPS - 2) * WIDTH), bf16)
    tail = jax.ShapeDtypeStruct((blocks, rows, WIDTH), bf16)
    high, low, *tails = local(
        complete_body, 24, [half, half, tail, tail], 1 << 31, 14 << 20,
        panel, inverses,
    )
    factor = [*factor, high, low]
    copies, own = local(second_body, 8, [group, tile], 1 << 27, 1 << 20, *tiles, *far, own, *factor)
    tiles = lax.all_to_all(copies, OWNERS, 0, 0)
    copies, own, packed = local(
        third_body, 8, [group, tile, shape(3 * TILES, members, rows)],
        1 << 27, 2 << 20, tiles, own, *factor,
    )
    early = crossings(packed, EARLY)
    received = lax.all_to_all(copies, OWNERS, 0, 0)
    ends = received[(STEPS - 1) * TILES:]
    late = crossings(ends, LATE)
    own, ends, *early = lax.optimization_barrier((own, ends, packed, *early))
    before, partly = local(
        middle_body, 16,
        [shape(members, (STEPS - 1) * WIDTH), shape(blocks, members, rows)],
        1 << 30, 12 << 20, *early, right, panel, inverses,
    )
    low, high, sums = local(
        finish_body, 16,
        [shape(blocks // 2, members, rows)] * 2 + [shape(2, blocks, rows)],
        1 << 28, 4 << 20, ends, *late, own, partly, *tails,
    )
    other = lax.ppermute(sums, "core", [(0, 1), (1, 0)])
    last, = local(
        last_body, 8, [shape(members, WIDTH)], 1 << 28, 1 << 20,
        ends, *late, inverses,
    )
    sums = sums + other
    for change in (1, 3):
        sums = sums + lax.ppermute(sums, "y", [(i, i ^ change) for i in range(4)])
    solved = jnp.concatenate([before, last], axis=1)
    left = jnp.concatenate([low, high], axis=0)
    size = members * 8
    mean = sums[0] / size
    spread = sums[1] / size - mean * mean
    return (
        solved.T,
        left.transpose(0, 2, 1).reshape(right_side.shape),
        spread.reshape(blocks, 1, rows),
    )


def solution(mesh):
    fine = Mesh(mesh.devices.reshape(SIZES), AXES)
    return jax.shard_map(
        shards,
        mesh=fine,
        in_specs=(P(None, ROWS, None, None), P(None, ROWS, None, MEM), P()),
        out_specs=(P(None, MEM), P(None, ROWS, None, MEM), P(None, ROWS, None)),
        check_vma=False,
    )
```
